32 devices in a mesh: seq: 4 (over y, x), req: 8 (over z, core).
Axes of the slice: x: 2, y: 2, z: 4, core: 2. Of those that a mesh axis runs over, the one named last changes fastest.
Arguments:
- hidden_in: bfloat16 [16, 256, 8192], P('req', 'seq'), may hold values from -6 to 6
- q_base: bfloat16 [16, 256, 1024], P('req', 'seq'), may hold values from -12 to 12
- kv_base: bfloat16 [16, 256, 256], P('req', 'seq'), may hold values from -6 to 6
- cache_kv: bfloat16 [16, 1024, 256], P('req', 'seq'), may hold values from -6 to 6
- req_adapter: int32 [16], replicated, may hold values from 0 to 7
- slot_of_adapter: int32 [8], replicated, may hold values from 0 to 7, each once
- down_panels: bfloat16 [8, 8192, 192], P('req', 'seq'), may hold values from -0.0625 to 0.0625
- up_panels: bfloat16 [8, 64, 2304], P('req', 'seq'), may hold values from -0.75 to 0.75
Outputs:
- attn_out: bfloat16 [16, 256, 1024], P('req', 'seq')
- o_low: float32 [16, 256, 64], P('req', 'seq')
- new_kv: bfloat16 [16, 256, 256], P('req', 'seq')
The draws below stay inside these ranges and needn't reach their ends.
Inputs may be any that keep to these rules, and one draw needn't show every extreme that they name: `req_adapter`: several requests may name the same adapter. `slot_of_adapter`: each adapter has its own slot.
All inputs are finite; a program needn't handle non-finite values.
Results may differ from the reference program's by a relative error of at most 0.012.
The reference program's roundings to bfloat16 on the way count: a program that leaves them out, or rounds other values in their place, can miss the bound.
Values may be sent and summed in bfloat16 or wider, within the bound.
A program may use at most 64 MiB of HBM per device.

```python
import math
import jax
import jax.numpy as jnp
import numpy as np
from jax import lax

D = 8192
HD = 128
HQ = 8
R = 64
REQS = 16
SPAN = 256
CTX = 1024
NADAPT = 8
QW = 1024
UPW = 2304


def draw_q_base(key, part):
    shape = (REQS, SPAN, HQ * HD)
    base = jnp.clip(jax.random.normal(jax.random.fold_in(key, 1), shape, jnp.float32), -6.0, 6.0)
    return base.astype(jnp.bfloat16)


def draw_cache_kv(key, part):
    shape = (REQS, CTX, 2 * HD)
    base = jnp.clip(jax.random.normal(jax.random.fold_in(key, 2), shape, jnp.float32), -6.0, 6.0)
    return base.astype(jnp.bfloat16)


def place_ends(values, key, least, top_value):
    extent = values.shape
    spot = [jax.random.randint(jax.random.fold_in(key, axis), (), 0, extent[axis]) for axis in range(len(extent))]
    values = values.at[tuple(spot)].set(least)
    longest = extent.index(max(extent))
    spot[longest] = (spot[longest] + 1) % extent[longest]
    return values.at[tuple(spot)].set(top_value)


def shard_levels(own_key, dims, split, least, top_value):
    loudness = 1.0
    for dim, parts in split:
        steps = jax.random.uniform(jax.random.fold_in(jax.random.fold_in(own_key, 6), dim), (parts,), jnp.float32, least / len(split), top_value / len(split))
        loudness = loudness * jnp.repeat(jnp.exp(steps), dims[dim] // parts).reshape((-1,) + (1,) * (len(dims) - 1 - dim))
    return loudness


def rank_table(number_of, lean):
    portions = [(1 << 20) // math.isqrt(rank ** lean) + 1 for rank in range(1, number_of + 1)]
    spread = 1 + sum(portions) // (1 << 30)
    return np.cumsum(np.array([max(1, weight // spread) for weight in portions]))


def ranked_ids(key, shape, amount, slope):
    listing = rank_table(amount, slope)
    pick = jax.random.randint(jax.random.fold_in(key, 1), shape, 0, int(listing[amount - 1]))
    grade = jnp.searchsorted(jnp.asarray(listing, jnp.int32), pick, side="right")
    return jax.random.permutation(jax.random.fold_in(key, 2), amount)[grade].astype(jnp.int32)


def normal_values(own_key, extent, spread, most, pieces=(), kind=jnp.bfloat16):
    factor_of = shard_levels(own_key, extent, pieces, -0.22, 0.18) if pieces else 1.0
    array = jax.random.normal(own_key, extent, jnp.float32) * spread * factor_of
    return jnp.minimum(jnp.maximum(array, -most), most).astype(kind)


def setup_inputs(seed: int = 0) -> dict:
    splits = jax.random.split(jax.random.key(seed), 9)
    hidden_in = normal_values(splits[0], (REQS, SPAN, D), 1.0, 6.0, ((0, 8), (1, 4)))
    q_base = draw_q_base(jax.random.fold_in(splits[8], 71), 0)
    kv_base = normal_values(splits[2], (REQS, SPAN, 2 * HD), 1.0, 6.0, ((0, 8), (1, 4)))
    cache_kv = draw_cache_kv(jax.random.fold_in(splits[8], 71), 0)
    req_adapter = place_ends(ranked_ids(splits[4], (REQS,), NADAPT, 2), jax.random.fold_in(splits[4], 3), 0, NADAPT - 1).astype(jnp.int32)
    slot_of_adapter = jax.random.permutation(splits[5], NADAPT).astype(jnp.int32)
    down_panels = normal_values(splits[6], (NADAPT, D, 3 * R), D ** -0.5, 0.0625, ((0, 8), (1, 4)))
    up_panels = normal_values(splits[7], (NADAPT, R, UPW), R ** -0.5, 0.75, ((0, 8), (1, 4)))
    return dict(hidden_in=hidden_in, q_base=q_base, kv_base=kv_base, cache_kv=cache_kv, req_adapter=req_adapter, slot_of_adapter=slot_of_adapter, down_panels=down_panels, up_panels=up_panels)


def rotate(vectors, positions):
    half_dim = vectors.shape[-1] // 2
    inverse = 500000.0 ** (-jnp.arange(half_dim, dtype=jnp.float32) / half_dim)
    angles = positions.astype(jnp.float32)[:, None] * inverse[None, :]
    cosine = jnp.cos(angles)[:, None, :]
    sine_part = jnp.sin(angles)[:, None, :]
    first_half = vectors[..., :half_dim]
    second_half = vectors[..., half_dim:]
    return jnp.concatenate([first_half * cosine - second_half * sine_part, second_half * cosine + first_half * sine_part], axis=-1)


def reference(hidden_in, q_base, kv_base, cache_kv, req_adapter, slot_of_adapter, down_panels, up_panels):
    slots = jnp.take(slot_of_adapter, req_adapter).astype(jnp.int32)

    def per_request(inputs):
        hidden, query_base, key_value, cached, slot_index = inputs
        down_panel = down_panels[slot_index]
        up_panel = up_panels[slot_index]
        low_rank = jnp.dot(hidden, down_panel, preferred_element_type=jnp.float32).astype(jnp.bfloat16)
        delta_q = jnp.dot(low_rank[:, :R], up_panel[:, :QW], preferred_element_type=jnp.float32)
        delta_k = jnp.dot(low_rank[:, R:2 * R], up_panel[:, QW:QW + HD], preferred_element_type=jnp.float32)
        delta_v = jnp.dot(low_rank[:, 2 * R:3 * R], up_panel[:, QW + HD:QW + 2 * HD], preferred_element_type=jnp.float32)
        positions = CTX + jnp.arange(SPAN, dtype=jnp.int32)
        queries = rotate((query_base.astype(jnp.float32) + delta_q).reshape(SPAN, HQ, HD), positions).astype(jnp.bfloat16)
        keys_new = rotate((key_value[:, :HD].astype(jnp.float32) + delta_k)[:, None, :], positions)[:, 0, :]
        values_new = key_value[:, HD:].astype(jnp.float32) + delta_v
        fresh_kv = jnp.concatenate([keys_new, values_new], axis=1).astype(jnp.bfloat16)
        all_keys = jnp.concatenate([cached[:, :HD], fresh_kv[:, :HD]], axis=0).astype(jnp.float32)
        all_values = jnp.concatenate([cached[:, HD:], fresh_kv[:, HD:]], axis=0).astype(jnp.float32)
        scores = jnp.einsum("thd,kd->htk", queries.astype(jnp.float32), all_keys) * (HD ** -0.5)
        key_index = jnp.arange(CTX + SPAN, dtype=jnp.int32)
        query_index = jnp.arange(SPAN, dtype=jnp.int32)
        visible = (key_index[None, :] < CTX) | ((key_index[None, :] - CTX) <= query_index[:, None])
        scores = jnp.where(visible[None], scores, -1e30)
        largest = jnp.max(scores, axis=-1, keepdims=True)
        weights = jnp.where(visible[None], jnp.exp(scores - largest), 0.0)
        denom = jnp.sum(weights, axis=-1)
        rounded = lax.optimization_barrier(weights.astype(jnp.bfloat16))
        mixed = jnp.einsum("htk,kd->thd", rounded.astype(jnp.float32), all_values)
        mixed = mixed / jnp.transpose(denom)[:, :, None]
        attention = mixed.reshape(SPAN, QW).astype(jnp.bfloat16)
        output_low = jnp.dot(attention, jnp.transpose(up_panel[:, QW + 2 * HD:]), preferred_element_type=jnp.float32)
        return attention, output_low, fresh_kv

    attn_out, o_low, new_kv = lax.map(per_request, (hidden_in, q_base, kv_base, cache_kv, slots))
    return (attn_out, o_low, new_kv)
```

```python
import functools

import jax
import jax.numpy as jnp
from jax import lax
from jax.experimental import pallas as pl
from jax.experimental.pallas import tpu as pltpu
from jax.sharding import PartitionSpec as P

masked_score = -1e30
MESH = pl.DeviceIdType.MESH


def rotate(vectors, positions):
    half_dim = vectors.shape[-1] // 2
    inverse = 500000.0 ** (-jnp.arange(half_dim, dtype=jnp.float32) / half_dim)
    angles = positions.astype(jnp.float32)[:, None] * inverse[None, :]
    cosine = jnp.cos(angles)[:, None, :]
    sine_part = jnp.sin(angles)[:, None, :]
    first_half = vectors[..., :half_dim]
    second_half = vectors[..., half_dim:]
    return jnp.concatenate(
        [
            first_half * cosine - second_half * sine_part,
            second_half * cosine + first_half * sine_part,
        ],
        axis=-1,
    )


def on_device(
    hidden_in, q_base, kv_base, cache_kv, req_adapter, slot_of_adapter, down_panels, up_panels
):
    requests, seg_rows, model_width = hidden_in.shape
    head_dim = kv_base.shape[2] // 2
    q_width = q_base.shape[2]
    head_count = q_width // head_dim
    rank_all = down_panels.shape[2]
    rank_size = rank_all // 3
    pre_rows = cache_kv.shape[1]
    seq_count = lax.axis_size("seq")
    seq_pos = lax.axis_index("seq")
    req_pos = lax.axis_index("req")
    context = pre_rows * seq_count
    my_adapters = lax.dynamic_slice_in_dim(req_adapter, req_pos * requests, requests)
    wanted = jnp.take(slot_of_adapter, my_adapters)
    pieces = (
        lax.all_gather(down_panels, "req", axis=0, tiled=True),
        lax.all_gather(up_panels, "req", axis=0, tiled=True),
    )
    slot_ids = jnp.arange(pieces[0].shape[0], dtype=jnp.int32)
    onehot = (wanted[:, None] == slot_ids[None, :]).astype(jnp.bfloat16)
    down_part = jnp.einsum("js,snc->jnc", onehot, pieces[0], preferred_element_type=jnp.float32)
    up_part = jnp.einsum("js,snc->jnc", onehot, pieces[1], preferred_element_type=jnp.float32)
    down_sel = down_part
    up_sel = up_part
    down_sel = down_sel.astype(jnp.bfloat16)
    up_sel = up_sel.astype(jnp.bfloat16)
    up_full = lax.all_gather(up_sel, "seq", axis=1, tiled=True)
    low_rank = jnp.einsum(
        "jtd,jdc->jtc",
        hidden_in,
        lax.all_gather(down_sel, "seq", axis=1, tiled=True),
        preferred_element_type=jnp.float32,
    )
    low_half = low_rank.astype(jnp.bfloat16)
    delta_q = jnp.einsum(
        "jtr,jrc->jtc",
        low_half[:, :, :rank_size],
        up_full[:, :, :q_width],
        preferred_element_type=jnp.float32,
    )
    delta_k = jnp.einsum(
        "jtr,jrc->jtc",
        low_half[:, :, rank_size : 2 * rank_size],
        up_full[:, :, q_width : q_width + head_dim],
        preferred_element_type=jnp.float32,
    )
    delta_v = jnp.einsum(
        "jtr,jrc->jtc",
        low_half[:, :, 2 * rank_size :],
        up_full[:, :, q_width + head_dim : q_width + 2 * head_dim],
        preferred_element_type=jnp.float32,
    )
    query_index = seq_pos * seg_rows + jnp.arange(seg_rows, dtype=jnp.int32)
    positions = context + query_index
    queries = rotate(
        (q_base.astype(jnp.float32) + delta_q).reshape(requests, seg_rows, head_count, head_dim),
        positions,
    ).astype(jnp.bfloat16)
    keys_new = rotate(
        (kv_base[:, :, :head_dim].astype(jnp.float32) + delta_k)[:, :, None, :], positions
    )[:, :, 0, :]
    values_new = kv_base[:, :, head_dim:].astype(jnp.float32) + delta_v
    new_kv = jnp.concatenate([keys_new, values_new], axis=2).astype(jnp.bfloat16)
    local_kv = jnp.concatenate([cache_kv, new_kv], axis=1)
    kv_rows = pre_rows + seg_rows
    score_scale = head_dim ** (-0.5)

    def attend_block(state_now, key_block, first_row):
        running_max, running_sum, weighted = state_now
        key_part = key_block[:, :, :head_dim]
        value_part = key_block[:, :, head_dim:]
        scores = (
            jnp.einsum("jthd,jkd->jhtk", queries, key_part, preferred_element_type=jnp.float32)
            * score_scale
        )
        global_index = first_row + jnp.arange(key_block.shape[1], dtype=jnp.int32)
        owner_dev = global_index // kv_rows
        offset = global_index % kv_rows
        span_index = owner_dev * seg_rows + offset - pre_rows
        visible = (offset[None, :] < pre_rows) | (span_index[None, :] <= query_index[:, None])
        scores = jnp.where(visible[None, None], scores, masked_score)
        newest = jnp.maximum(running_max, jnp.max(scores, axis=-1))
        weights = jnp.where(visible[None, None], jnp.exp(scores - newest[..., None]), 0.0)
        factor = jnp.exp(running_max - newest)
        running_sum = running_sum * factor + jnp.sum(weights, axis=-1)
        weighted = weighted * factor[..., None] + jnp.einsum(
            "jhtk,jkd->jhtd",
            weights.astype(jnp.bfloat16),
            value_part,
            preferred_element_type=jnp.float32,
        )
        return (newest, running_sum, weighted)

    start_state = (
        jnp.full((requests, head_count, seg_rows), masked_score, jnp.float32),
        jnp.zeros((requests, head_count, seg_rows), jnp.float32),
        jnp.zeros((requests, head_count, seg_rows, head_dim), jnp.float32),
    )
    kv_piece = lax.all_gather(local_kv, "seq", axis=1, tiled=True)
    piece_rows = kv_piece.shape[1]

    def advance(block_number, state_inner):
        key_block = lax.dynamic_slice_in_dim(kv_piece, block_number * kv_rows, kv_rows, 1)
        return attend_block(state_inner, key_block, block_number * kv_rows)

    running_max, running_sum, weighted = lax.fori_loop(
        0, piece_rows // kv_rows, advance, start_state
    )
    mixed = weighted / running_sum[..., None]
    attn_out = (
        jnp.transpose(mixed, (0, 2, 1, 3)).reshape(requests, seg_rows, q_width).astype(jnp.bfloat16)
    )
    o_low = jnp.einsum(
        "jtc,jrc->jtr",
        attn_out,
        up_full[:, :, q_width + 2 * head_dim :],
        preferred_element_type=jnp.float32,
    )
    return (attn_out, o_low, new_kv)

def attend_kernel(
    z_count,
    req_adapter,
    slot_of_adapter,
    hidden_in,
    down_in,
    up_in,
    cache_in,
    q_base,
    kv_base,
    cos_in,
    sin_in,
    attn_out,
    o_low,
    new_kv,
    hid,
    down_all,
    down_end,
    up_all,
    up_sel,
    up_got,
    kv_all,
    kv_new,
    part,
    part_got,
    part_end,
    end_got,
    queries,
    acc,
    top,
    total,
    local_sem,
    hid_send,
    hid_recv,
    kv_send,
    kv_recv,
    up_send,
    up_recv,
    part_send,
    part_recv,
    end_send,
    end_recv,
    new_send,
    new_recv,
    z_send,
    z_recv,
    mate_send,
    mate_recv,
):
    requests, rows, _ = q_base.shape
    seq_count, _, _, depth = hid.shape
    head_dim = kv_base.shape[2] // 2
    q_width = q_base.shape[2]
    head_count = q_width // head_dim
    rank = head_dim // 2
    pre_rows = cache_in.shape[1]
    span = seq_count * rows
    seq = lax.axis_index("seq")
    req = lax.axis_index("req")
    z = req // 2
    core = req % 2
    mate = {"req": z * 2 + (1 - core)}
    ahead = {"req": req + 2}
    behind = {"req": req - 2}
    peers = [lax.rem(seq + k, seq_count) for k in range(seq_count)]

    def send(src, dst, s_sem, r_sem, target):
        return pltpu.make_async_remote_copy(
            src_ref=src,
            dst_ref=dst,
            send_sem=s_sem,
            recv_sem=r_sem,
            device_id=target,
            device_id_type=MESH,
        )

    held = (up_all, down_all, down_end)
    own = (up_in, down_in.at[pl.ds(0, head_dim)], down_in.at[pl.ds(head_dim, rank)])
    local = [
        pltpu.make_async_copy(hidden_in.at[:, :, pl.ds(seq * depth, depth)], hid.at[seq], local_sem.at[0]),
        pltpu.make_async_copy(cache_in, kv_all.at[:, pl.ds(seq * pre_rows, pre_rows), :], local_sem.at[1]),
        pltpu.make_async_copy(own[1], down_all.at[req], local_sem.at[2]),
        pltpu.make_async_copy(own[2], down_end.at[req], local_sem.at[3]),
        pltpu.make_async_copy(own[0], up_all.at[req], local_sem.at[4]),
    ]
    for copy in local:
        copy.start()

    barrier = pltpu.get_barrier_semaphore()
    for k in range(1, seq_count):
        pl.semaphore_signal(barrier, inc=1, device_id={"seq": peers[k]}, device_id_type=MESH)
    pl.semaphore_signal(barrier, inc=1, device_id=mate, device_id_type=MESH)

    @pl.when(z > 0)
    def _():
        pl.semaphore_signal(barrier, inc=1, device_id=behind, device_id_type=MESH)

    @pl.when(z < z_count - 1)
    def _():
        pl.semaphore_signal(barrier, inc=1, device_id=ahead, device_id_type=MESH)

    ends = (z > 0).astype(jnp.int32) + (z < z_count - 1).astype(jnp.int32)
    pl.semaphore_wait(barrier, seq_count + ends)

    def along(way, step, kind, chip, src=None):
        slot = chip * 2 + core
        return send(
            held[kind].at[slot] if src is None else src,
            held[kind].at[slot],
            z_send.at[way, step, kind],
            z_recv.at[way, step, kind],
            ahead if way == 0 else behind,
        )

    def across(kind, chip, src=None):
        slot = chip * 2 + core
        return send(
            held[kind].at[slot] if src is None else src,
            held[kind].at[slot],
            mate_send.at[kind, chip],
            mate_recv.at[kind, chip],
            mate,
        )

    def can_send(way, step):
        if way == 0:
            return (z < z_count - 1) & (z - step >= 0)
        return (z > 0) & (z + step <= z_count - 1)

    def can_get(way, step):
        return z - 1 - step >= 0 if way == 0 else z + 1 + step <= z_count - 1

    def passed(way, step):
        return z - step if way == 0 else z + step

    for way in range(2):

        @pl.when(can_send(way, 0))
        def _(way=way):
            for kind in range(3):
                along(way, 0, kind, z, own[kind]).start()

    for kind in range(3):
        across(kind, z, own[kind]).start()

    def hid_copy(k):
        return send(
            hidden_in.at[:, :, pl.ds(peers[k] * depth, depth)],
            hid.at[seq],
            hid_send.at[k],
            hid_recv.at[k],
            {"seq": peers[k]},
        )

    def kv_copy(k):
        return send(
            cache_in,
            kv_all.at[:, pl.ds(seq * pre_rows, pre_rows), :],
            kv_send.at[k],
            kv_recv.at[k],
            {"seq": peers[k]},
        )

    def up_copy(k):
        return send(up_sel, up_got.at[seq], up_send.at[k], up_recv.at[k], {"seq": peers[k]})

    def part_copy(k):
        return send(
            part.at[peers[k]], part_got.at[k], part_send.at[k], part_recv.at[k], {"seq": peers[k]}
        )

    def end_copy(k):
        return send(
            part_end.at[peers[k]], end_got.at[k], end_send.at[k], end_recv.at[k], {"seq": peers[k]}
        )

    def new_copy(k):
        here = kv_new.at[:, pl.ds(seq * rows, rows), :]
        return send(here, here, new_send.at[k], new_recv.at[k], {"seq": peers[k]})

    others = range(1, seq_count)
    for k in others:
        hid_copy(k).start()
    for k in others:
        kv_copy(k).start()

    def relay(step, kind):
        for way in range(2):

            @pl.when(can_get(way, step))
            def _(way=way):
                chip = passed(way, step + 1)
                along(way, step, kind, chip).wait_recv()
                across(kind, chip).start()

            if step + 1 < z_count - 1:

                @pl.when(can_send(way, step + 1))
                def _(way=way):
                    along(way, step + 1, kind, passed(way, step + 1)).start()

    for step in range(z_count - 1):
        relay(step, 0)
        if step < z_count - 2:
            relay(step, 1)
            relay(step, 2)

    wanted = [slot_of_adapter[req_adapter[req * requests + j]] for j in range(requests)]
    local[4].wait()
    for chip in range(z_count):
        across(0, chip).wait_recv()
    for j in range(requests):
        up_sel[j] = up_all[wanted[j]]
    for k in others:
        up_copy(k).start()
    relay(z_count - 2, 1)
    for j in range(requests):
        up_got[seq, j] = up_sel[j]
    for copy in local[:4]:
        copy.wait()
    for k in others:
        hid_copy(k).wait_recv()
    for chip in range(z_count):
        across(1, chip).wait_recv()

    contract = (((1,), (1,)), ((), ()))
    for j in range(requests):
        h = hid[:, j].reshape(span, depth)
        thick = lax.dot_general(h, down_all[wanted[j]], contract, preferred_element_type=jnp.float32)
        for s in range(seq_count):
            part[s, j * rows : (j + 1) * rows, :] = thick[s * rows : (s + 1) * rows]
    for k in others:
        part_copy(k).start()
    relay(z_count - 2, 2)

    for k in others:
        up_copy(k).wait_recv()
    for k in others:
        part_copy(k).wait_recv()
    low = part[seq]
    for k in others:
        low = low + part_got[k]
    low = low.astype(jnp.bfloat16)
    cosine = cos_in[...]
    sine = sin_in[...]

    def rotated(u):
        return u * cosine + pltpu.roll(u, rank, 1) * sine

    ups = [up_got[:, j].reshape(rank, up_got.shape[3]) for j in range(requests)]
    for j in range(requests):
        low_q = low[j * rows : (j + 1) * rows, :rank]
        delta_q = jnp.dot(low_q, ups[j][:, :q_width], preferred_element_type=jnp.float32)
        for h in range(head_count):
            cols = slice(h * head_dim, (h + 1) * head_dim)
            u = q_base[j, :, cols].astype(jnp.float32) + delta_q[:, cols]
            queries[j, h * rows : (h + 1) * rows, :] = rotated(u).astype(jnp.bfloat16)

    for chip in range(z_count):
        across(2, chip).wait_recv()
    thin = []
    for j in range(requests):
        h = hid[:, j].reshape(span, depth)
        thin.append(
            lax.dot_general(h, down_end[wanted[j]], contract, preferred_element_type=jnp.float32)
        )
    joined = jnp.concatenate(thin, axis=1)
    for s in range(seq_count):
        part_end[s] = joined[s * rows : (s + 1) * rows]
    for k in others:
        end_copy(k).start()

    for k in others:
        kv_copy(k).wait_recv()
    scale = head_dim ** (-0.5)
    group = 4 * rows

    def extend():
        for k in others:
            end_copy(k).wait_recv()
        low_end = part_end[seq]
        for k in others:
            low_end = low_end + end_got[k]
        low_end = low_end.astype(jnp.bfloat16)
        for j in range(requests):
            low_k = low[j * rows : (j + 1) * rows, rank:]
            low_v = low_end[:, j * rank : (j + 1) * rank]
            up = ups[j]
            delta_k = jnp.dot(low_k, up[:, q_width : q_width + head_dim], preferred_element_type=jnp.float32)
            delta_v = jnp.dot(
                low_v,
                up[:, q_width + head_dim : q_width + 2 * head_dim],
                preferred_element_type=jnp.float32,
            )
            base = kv_base[j].astype(jnp.float32)
            key = rotated(base[:, :head_dim] + delta_k).astype(jnp.bfloat16)
            value = (base[:, head_dim:] + delta_v).astype(jnp.bfloat16)
            fresh = jnp.concatenate([key, value], axis=1)
            new_kv[j] = fresh
            kv_new[j, pl.ds(seq * rows, rows), :] = fresh
        for k in others:
            new_copy(k).start()

    for j in range(requests):
        for g in range(head_count * rows // group):
            at = slice(g * group, (g + 1) * group)
            scores = (
                lax.dot_general(
                    queries[j, at, :],
                    kv_all[j, :, :head_dim],
                    contract,
                    preferred_element_type=jnp.float32,
                )
                * scale
            )
            m = jnp.max(scores, axis=1, keepdims=True)
            w = jnp.exp(scores - m)
            top[j, at, :] = jnp.broadcast_to(m, (group, head_dim))
            total[j, at, :] = jnp.broadcast_to(jnp.sum(w, axis=1, keepdims=True), (group, head_dim))
            acc[j, at, :] = jnp.dot(
                w.astype(jnp.bfloat16), kv_all[j, :, head_dim:], preferred_element_type=jnp.float32
            )
        if j == 0:
            extend()

    for k in others:
        new_copy(k).wait_recv()
    token = lax.rem(lax.broadcasted_iota(jnp.int32, (group, span), 0), rows) + seq * rows
    visible = lax.broadcasted_iota(jnp.int32, (group, span), 1) <= token
    for j in range(requests):
        heads = []
        for g in range(head_count * rows // group):
            at = slice(g * group, (g + 1) * group)
            scores = (
                lax.dot_general(
                    queries[j, at, :],
                    kv_new[j, :, :head_dim],
                    contract,
                    preferred_element_type=jnp.float32,
                )
                * scale
            )
            scores = jnp.where(visible, scores, masked_score)
            old = top[j, at, :]
            m = jnp.maximum(old, jnp.max(scores, axis=1, keepdims=True))
            w = jnp.exp(scores - m[:, :1])
            factor = jnp.exp(old - m)
            denom = total[j, at, :] * factor + jnp.sum(w, axis=1, keepdims=True)
            mixed = acc[j, at, :] * factor + jnp.dot(
                w.astype(jnp.bfloat16), kv_new[j, :, head_dim:], preferred_element_type=jnp.float32
            )
            mixed = (mixed / denom).astype(jnp.bfloat16)
            for i in range(group // rows):
                heads.append(mixed[i * rows : (i + 1) * rows])
        attention = jnp.concatenate(heads, axis=1)
        attn_out[j] = attention
        o_low[j] = lax.dot_general(
            attention, ups[j][:, q_width + 2 * head_dim :], contract, preferred_element_type=jnp.float32
        )

    for k in others:
        for copy in (hid_copy(k), kv_copy(k), up_copy(k), part_copy(k), end_copy(k), new_copy(k)):
            copy.wait_send()
    for kind in range(3):
        for chip in range(z_count):
            across(kind, chip).wait_send()
        for way in range(2):
            for step in range(z_count - 1):

                @pl.when(can_send(way, step))
                def _(way=way, step=step, kind=kind):
                    along(way, step, kind, passed(way, step)).wait_send()


def fused(
    hidden_in, q_base, kv_base, cache_kv, req_adapter, slot_of_adapter, down_panels, up_panels
):
    requests, rows, _ = hidden_in.shape
    head_dim = kv_base.shape[2] // 2
    q_width = q_base.shape[2]
    pre_rows = cache_kv.shape[1]
    seq_count = lax.axis_size("seq")
    req_count = lax.axis_size("req")
    depth = down_panels.shape[1]
    rank_rows, up_width = up_panels.shape[1:]
    z_count = req_count // 2
    half_dim = head_dim // 2
    panel = down_panels[0].T
    positions = (
        pre_rows * seq_count
        + lax.axis_index("seq") * rows
        + jnp.arange(rows, dtype=jnp.int32)
    )
    inverse = 500000.0 ** (-jnp.arange(half_dim, dtype=jnp.float32) / half_dim)
    angles = positions.astype(jnp.float32)[:, None] * inverse[None, :]
    cosine = jnp.cos(angles)
    sine = jnp.sin(angles)
    cosine = jnp.concatenate([cosine, cosine], axis=1)
    sine = jnp.concatenate([-sine, sine], axis=1)
    span = seq_count * rows
    q_rows = q_width // head_dim * rows
    bf16, f32 = jnp.bfloat16, jnp.float32
    dma = pltpu.SemaphoreType.DMA
    smem = pl.BlockSpec(memory_space=pltpu.SMEM)
    vmem = pl.BlockSpec(memory_space=pltpu.VMEM)
    anywhere = pl.BlockSpec(memory_space=pltpu.HBM)
    return pl.pallas_call(
        functools.partial(attend_kernel, z_count),
        out_shape=(
            jax.ShapeDtypeStruct((requests, rows, q_width), bf16),
            jax.ShapeDtypeStruct((requests, rows, half_dim), f32),
            jax.ShapeDtypeStruct((requests, rows, 2 * head_dim), bf16),
        ),
        in_specs=[smem, smem, anywhere, anywhere, anywhere, anywhere, vmem, vmem, vmem, vmem],
        out_specs=(vmem, vmem, vmem),
        scratch_shapes=[
            pltpu.VMEM((seq_count, requests, rows, depth), bf16),
            pltpu.VMEM((req_count, head_dim, depth), bf16),
            pltpu.VMEM((req_count, half_dim, depth), bf16),
            pltpu.VMEM((req_count, rank_rows, up_width), bf16),
            pltpu.VMEM((requests, rank_rows, up_width), bf16),
            pltpu.VMEM((seq_count, requests, rank_rows, up_width), bf16),
            pltpu.VMEM((requests, seq_count * pre_rows, 2 * head_dim), bf16),
            pltpu.VMEM((requests, span, 2 * head_dim), bf16),
            pltpu.VMEM((seq_count, requests * rows, head_dim), f32),
            pltpu.VMEM((seq_count, requests * rows, head_dim), f32),
            pltpu.VMEM((seq_count, rows, head_dim), f32),
            pltpu.VMEM((seq_count, rows, head_dim), f32),
            pltpu.VMEM((requests, q_rows, head_dim), bf16),
            pltpu.VMEM((requests, q_rows, head_dim), f32),
            pltpu.VMEM((requests, q_rows, head_dim), f32),
            pltpu.VMEM((requests, q_rows, head_dim), f32),
            dma((5,)),
        ]
        + [dma((seq_count,))] * 12
        + [dma((2, z_count - 1, 3))] * 2
        + [dma((3, z_count))] * 2,
        compiler_params=pltpu.CompilerParams(
            collective_id=0, has_side_effects=True, vmem_limit_bytes=48 * 1024 * 1024
        ),
    )(
        *[
            pltpu.with_memory_space_constraint(a, pltpu.HBM)
            for a in (
                req_adapter,
                slot_of_adapter,
                hidden_in,
                panel,
                up_panels[0],
                cache_kv,
                q_base,
                kv_base,
            )
        ],
        cosine,
        sine,
    )


def fits(mesh):
    return mesh.shape["req"] % 2 == 0 and mesh.shape["seq"] <= 4


def solution(mesh):
    return jax.shard_map(
        fused if fits(mesh) else on_device,
        mesh=mesh,
        in_specs=(
            P("req", "seq", None),
            P("req", "seq", None),
            P("req", "seq", None),
            P("req", "seq", None),
            P(),
            P(),
            P("req", "seq", None),
            P("req", "seq", None),
        ),
        out_specs=(P("req", "seq", None), P("req", "seq", None), P("req", "seq", None)),
        check_vma=False,
    )
```

```python
import functools

import jax
import jax.numpy as jnp
from jax import lax
from jax.experimental import pallas as pl
from jax.experimental.pallas import tpu as pltpu
from jax.sharding import PartitionSpec as P

masked_score = -1e30
MESH = pl.DeviceIdType.MESH


def rotate(vectors, positions):
    half_dim = vectors.shape[-1] // 2
    inverse = 500000.0 ** (-jnp.arange(half_dim, dtype=jnp.float32) / half_dim)
    angles = positions.astype(jnp.float32)[:, None] * inverse[None, :]
    cosine = jnp.cos(angles)[:, None, :]
    sine_part = jnp.sin(angles)[:, None, :]
    first_half = vectors[..., :half_dim]
    second_half = vectors[..., half_dim:]
    return jnp.concatenate(
        [
            first_half * cosine - second_half * sine_part,
            second_half * cosine + first_half * sine_part,
        ],
        axis=-1,
    )


def on_device(
    hidden_in, q_base, kv_base, cache_kv, req_adapter, slot_of_adapter, down_panels, up_panels
):
    requests, seg_rows, model_width = hidden_in.shape
    head_dim = kv_base.shape[2] // 2
    q_width = q_base.shape[2]
    head_count = q_width // head_dim
    rank_all = down_panels.shape[2]
    rank_size = rank_all // 3
    pre_rows = cache_kv.shape[1]
    seq_count = lax.axis_size("seq")
    seq_pos = lax.axis_index("seq")
    req_pos = lax.axis_index("req")
    context = pre_rows * seq_count
    my_adapters = lax.dynamic_slice_in_dim(req_adapter, req_pos * requests, requests)
    wanted = jnp.take(slot_of_adapter, my_adapters)
    pieces = (
        lax.all_gather(down_panels, "req", axis=0, tiled=True),
        lax.all_gather(up_panels, "req", axis=0, tiled=True),
    )
    slot_ids = jnp.arange(pieces[0].shape[0], dtype=jnp.int32)
    onehot = (wanted[:, None] == slot_ids[None, :]).astype(jnp.bfloat16)
    down_part = jnp.einsum("js,snc->jnc", onehot, pieces[0], preferred_element_type=jnp.float32)
    up_part = jnp.einsum("js,snc->jnc", onehot, pieces[1], preferred_element_type=jnp.float32)
    down_sel = down_part
    up_sel = up_part
    down_sel = down_sel.astype(jnp.bfloat16)
    up_sel = up_sel.astype(jnp.bfloat16)
    up_full = lax.all_gather(up_sel, "seq", axis=1, tiled=True)
    low_rank = jnp.einsum(
        "jtd,jdc->jtc",
        hidden_in,
        lax.all_gather(down_sel, "seq", axis=1, tiled=True),
        preferred_element_type=jnp.float32,
    )
    low_half = low_rank.astype(jnp.bfloat16)
    delta_q = jnp.einsum(
        "jtr,jrc->jtc",
        low_half[:, :, :rank_size],
        up_full[:, :, :q_width],
        preferred_element_type=jnp.float32,
    )
    delta_k = jnp.einsum(
        "jtr,jrc->jtc",
        low_half[:, :, rank_size : 2 * rank_size],
        up_full[:, :, q_width : q_width + head_dim],
        preferred_element_type=jnp.float32,
    )
    delta_v = jnp.einsum(
        "jtr,jrc->jtc",
        low_half[:, :, 2 * rank_size :],
        up_full[:, :, q_width + head_dim : q_width + 2 * head_dim],
        preferred_element_type=jnp.float32,
    )
    query_index = seq_pos * seg_rows + jnp.arange(seg_rows, dtype=jnp.int32)
    positions = context + query_index
    queries = rotate(
        (q_base.astype(jnp.float32) + delta_q).reshape(requests, seg_rows, head_count, head_dim),
        positions,
    ).astype(jnp.bfloat16)
    keys_new = rotate(
        (kv_base[:, :, :head_dim].astype(jnp.float32) + delta_k)[:, :, None, :], positions
    )[:, :, 0, :]
    values_new = kv_base[:, :, head_dim:].astype(jnp.float32) + delta_v
    new_kv = jnp.concatenate([keys_new, values_new], axis=2).astype(jnp.bfloat16)
    local_kv = jnp.concatenate([cache_kv, new_kv], axis=1)
    kv_rows = pre_rows + seg_rows
    score_scale = head_dim ** (-0.5)

    def attend_block(state_now, key_block, first_row):
        running_max, running_sum, weighted = state_now
        key_part = key_block[:, :, :head_dim]
        value_part = key_block[:, :, head_dim:]
        scores = (
            jnp.einsum("jthd,jkd->jhtk", queries, key_part, preferred_element_type=jnp.float32)
            * score_scale
        )
        global_index = first_row + jnp.arange(key_block.shape[1], dtype=jnp.int32)
        owner_dev = global_index // kv_rows
        offset = global_index % kv_rows
        span_index = owner_dev * seg_rows + offset - pre_rows
        visible = (offset[None, :] < pre_rows) | (span_index[None, :] <= query_index[:, None])
        scores = jnp.where(visible[None, None], scores, masked_score)
        newest = jnp.maximum(running_max, jnp.max(scores, axis=-1))
        weights = jnp.where(visible[None, None], jnp.exp(scores - newest[..., None]), 0.0)
        factor = jnp.exp(running_max - newest)
        running_sum = running_sum * factor + jnp.sum(weights, axis=-1)
        weighted = weighted * factor[..., None] + jnp.einsum(
            "jhtk,jkd->jhtd",
            weights.astype(jnp.bfloat16),
            value_part,
            preferred_element_type=jnp.float32,
        )
        return (newest, running_sum, weighted)

    start_state = (
        jnp.full((requests, head_count, seg_rows), masked_score, jnp.float32),
        jnp.zeros((requests, head_count, seg_rows), jnp.float32),
        jnp.zeros((requests, head_count, seg_rows, head_dim), jnp.float32),
    )
    kv_piece = lax.all_gather(local_kv, "seq", axis=1, tiled=True)
    piece_rows = kv_piece.shape[1]

    def advance(block_number, state_inner):
        key_block = lax.dynamic_slice_in_dim(kv_piece, block_number * kv_rows, kv_rows, 1)
        return attend_block(state_inner, key_block, block_number * kv_rows)

    running_max, running_sum, weighted = lax.fori_loop(
        0, piece_rows // kv_rows, advance, start_state
    )
    mixed = weighted / running_sum[..., None]
    attn_out = (
        jnp.transpose(mixed, (0, 2, 1, 3)).reshape(requests, seg_rows, q_width).astype(jnp.bfloat16)
    )
    o_low = jnp.einsum(
        "jtc,jrc->jtr",
        attn_out,
        up_full[:, :, q_width + 2 * head_dim :],
        preferred_element_type=jnp.float32,
    )
    return (attn_out, o_low, new_kv)

def attend_kernel(
    chunks,
    phases,
    req_adapter,
    slot_of_adapter,
    hidden_in,
    down_in,
    up_in,
    cache_in,
    q_base,
    kv_base,
    cos_in,
    sin_in,
    attn_out,
    o_low,
    new_kv,
    hid,
    up_sel,
    up_got,
    kv_all,
    key_new,
    value_new,
    part,
    part_got,
    queries,
    acc,
    top,
    total,
    fresh,
    local_sem,
    z_send,
    z_recv,
    mate_send,
    mate_recv,
    hid_send,
    hid_recv,
    kv_send,
    kv_recv,
    up_send,
    up_recv,
    part_send,
    part_recv,
    new_send,
    new_recv,
    *panels,
):
    requests, rows, _ = q_base.shape
    seq_count, _, _, depth = hid.shape
    head_dim = kv_base.shape[2] // 2
    q_width = q_base.shape[2]
    head_count = q_width // head_dim
    rank = head_dim // 2
    pre_rows = cache_in.shape[1]
    up_rows = up_in.shape[0]
    span = seq_count * rows
    count = len(chunks) + 1
    bufs, stages = panels[:count], (None,) + panels[count:]
    seq = lax.axis_index("seq")
    req = lax.axis_index("req")
    z = req // 2
    core = req % 2
    at_end = (z == 0) | (z == 3)
    inner = jnp.logical_not(at_end)
    left = z < 2
    first = jnp.where(z == 0, 1, jnp.where(z == 1, 0, jnp.where(z == 2, 3, 2)))
    second = jnp.where(at_end, 3 - first, 3 - z)
    third = jnp.where(at_end, 3 - z, 3 - first)
    chips = (z, first, second, third)
    slots = [chip * 2 + core for chip in chips]
    land = jnp.where(left, 2, 0)
    mate = {"req": z * 2 + (1 - core)}
    to_first = {"req": slots[1]}
    to_second = {"req": slots[2]}
    peers = [seq, seq + 1 - 2 * (seq % 2), (seq + 2) % 4, 3 - seq]
    others = range(1, seq_count)

    def send(src, dst, s_sem, r_sem, target):
        return pltpu.make_async_remote_copy(
            src_ref=src,
            dst_ref=dst,
            send_sem=s_sem,
            recv_sem=r_sem,
            device_id=target,
            device_id_type=MESH,
        )

    starts = [sum(chunks[:i]) for i in range(len(chunks))]
    own = [up_in] + [down_in.at[pl.ds(a, n)] for a, n in zip(starts, chunks)]
    local = [pltpu.make_async_copy(own[p], bufs[p].at[slots[0]], local_sem.at[p]) for p in range(count)]
    local.append(
        pltpu.make_async_copy(
            hidden_in.at[:, :, pl.ds(seq * depth, depth)], hid.at[seq], local_sem.at[count]
        )
    )
    local.append(
        pltpu.make_async_copy(
            cache_in, kv_all.at[:, pl.ds(seq * pre_rows, pre_rows), :], local_sem.at[count + 1]
        )
    )

    barrier = pltpu.get_barrier_semaphore()
    for k in others:
        pl.semaphore_signal(barrier, inc=1, device_id={"seq": peers[k]}, device_id_type=MESH)
    pl.semaphore_signal(barrier, inc=1, device_id=mate, device_id_type=MESH)
    pl.semaphore_signal(barrier, inc=1, device_id=to_first, device_id_type=MESH)

    @pl.when(inner)
    def _():
        pl.semaphore_signal(barrier, inc=1, device_id=to_second, device_id_type=MESH)

    for copy in local:
        copy.start()
    pl.semaphore_wait(barrier, seq_count + 1 + inner.astype(jnp.int32))

    def z_copy(kind, p, chip, target, src=None):
        here = bufs[p].at[slots[chip]]
        return send(here if src is None else src, here, z_send.at[kind, p], z_recv.at[kind, p], target)

    def z_sel(p, target):
        return send(
            stages[p], bufs[p].at[pl.ds(land, requests)], z_send.at[3, p], z_recv.at[3, p], target
        )

    def across(p, chip, src=None):
        here = bufs[p].at[slots[chip]]
        return send(
            here if src is None else src, here, mate_send.at[chip, p], mate_recv.at[chip, p], mate
        )

    def hid_copy(k):
        return send(
            hidden_in.at[:, :, pl.ds(peers[k] * depth, depth)],
            hid.at[seq],
            hid_send.at[k],
            hid_recv.at[k],
            {"seq": peers[k]},
        )

    def spread(src, dst, size, sems, j, k):
        at = pl.ds(pl.multiple_of(seq * size, size), size)
        return send(src.at[j], dst.at[j, at], sems[0].at[j, k], sems[1].at[j, k], {"seq": peers[k]})

    def pass_on(dst, size, sems, j):
        here = dst.at[j, pl.ds(pl.multiple_of(peers[1 + j] * size, size), size)]
        return send(here, here, sems[0].at[j, 3], sems[1].at[j, 3], {"seq": peers[2 - j]})

    kv_args = (kv_all, pre_rows, (kv_send, kv_recv))
    up_args = (up_got, up_rows, (up_send, up_recv))

    def part_copy(phase, k):
        return send(
            part.at[phase, peers[k]],
            part_got.at[phase, k],
            part_send.at[phase, k],
            part_recv.at[phase, k],
            {"seq": peers[k]},
        )

    def new_copy(kind, k):
        ref = (key_new, value_new)[kind]
        here = ref.at[:, pl.ds(pl.multiple_of(seq * rows, rows), rows), :]
        return send(here, here, new_send.at[kind, k], new_recv.at[kind, k], {"seq": peers[k]})

    @pl.when(at_end)
    def _():
        for p in range(count):
            z_copy(0, p, 0, to_first, own[p]).start()

    @pl.when(inner)
    def _():
        z_copy(1, 0, 0, to_second, own[0]).start()
        z_copy(3, 0, 0, to_first, own[0]).start()
        z_copy(1, 1, 0, to_second, own[1]).start()

    for k in others:
        hid_copy(k).start()
    for p in range(count):
        across(p, 0, own[p]).start()

    wanted = [slot_of_adapter[req_adapter[req * requests + j]] for j in range(requests)]
    mine = [
        jnp.where(at_end & (w // 2 != z), land + j, w) for j, w in enumerate(wanted)
    ]

    def relay(p):
        @pl.when(inner)
        def _():
            z_copy(0, p, 1, to_first).wait_recv()
            z_copy(2, p, 1, to_second).start()
            across(p, 1).start()
            if p + 2 < count:
                z_copy(1, p + 2, 0, to_second, own[p + 2]).start()

    def finish_inner(p):
        @pl.when(inner)
        def _():
            z_copy(1, p, 2, to_second).wait_recv()
            across(p, 2).start()
            if p == 0:
                z_copy(4, p, 2, to_first).start()
            z_copy(2, p, 3, to_second).wait_recv()
            across(p, 3).start()
            if p == 0:
                z_copy(5, p, 3, to_first).start()
            local[p].wait()
            for chip in range(4):
                across(p, chip).wait_recv()
            if p > 0:
                for j in range(requests):
                    w = slot_of_adapter[req_adapter[slots[1] * requests + j]]
                    w = jnp.where(w // 2 == first, slots[0], w)
                    stages[p][j] = bufs[p][w]
                z_sel(p, to_first).start()

    def finish_end(p):
        @pl.when(at_end)
        def _():
            if p == 0:
                for kind in range(3):
                    z_copy(3 + kind, p, 1 + kind, to_first).wait_recv()
                    across(p, 1 + kind).start()
            else:
                z_sel(p, to_first).wait_recv()
            local[p].wait()
            for chip in range(4 if p == 0 else 1):
                across(p, chip).wait_recv()

    contract = (((1,), (1,)), ((), ()))

    def low_parts(phase):
        thin = []
        for j in range(requests):
            panel = jnp.concatenate([bufs[p][mine[j]] for p in phases[phase]], axis=0)
            h = hid[:, j].reshape(span, depth)
            thin.append(lax.dot_general(h, panel, contract, preferred_element_type=jnp.float32))
        joined = jnp.concatenate(thin, axis=1)
        for s in range(seq_count):
            part[phase, s] = joined[s * rows : (s + 1) * rows]
        for k in others:
            part_copy(phase, k).start()

    def low_of(phase):
        for k in others:
            part_copy(phase, k).wait_recv()
        low = part[phase, seq]
        for k in others:
            low = low + part_got[phase, k]
        low = jnp.concatenate([low] * requests, axis=0)
        row = lax.broadcasted_iota(jnp.int32, low.shape, 0) // rows
        lane = lax.broadcasted_iota(jnp.int32, low.shape, 1) // rank
        return jnp.where(row == lane, low, 0.0).astype(jnp.bfloat16)

    def up_cols(begin, size):
        return up_got[:, :, begin : begin + size].reshape(requests * rank, size)

    cosine = cos_in[...]
    sine = sin_in[...]

    def rotated(u):
        return u * cosine + pltpu.roll(u, rank, 1) * sine

    scale = head_dim ** (-0.5) * 1.4426950408889634
    group = 4 * rows
    groups = range(head_count * rows // group)

    def cached(j, g):
        at = slice(g * group, (g + 1) * group)
        scores = (
            lax.dot_general(
                queries[j, at, :], kv_all[j, :, :head_dim], contract, preferred_element_type=jnp.float32
            )
            * scale
        )
        m = jnp.max(scores, axis=1, keepdims=True)
        w = jnp.exp2(scores - m)
        top[j, at, :] = jnp.broadcast_to(m, (group, head_dim))
        total[j, at, :] = jnp.broadcast_to(jnp.sum(w, axis=1, keepdims=True), (group, head_dim))
        acc[j, at, :] = jnp.dot(
            w.astype(jnp.bfloat16), kv_all[j, :, head_dim:], preferred_element_type=jnp.float32
        )

    relay(0)
    relay(1)
    finish_inner(0)
    finish_end(0)
    for j in range(requests):
        up_sel[j] = bufs[0][wanted[j]]
    for j in range(requests):
        for k in (1, 2):
            spread(up_sel, *up_args, j, k).start()
        up_got[j, pl.ds(pl.multiple_of(seq * up_rows, up_rows), up_rows)] = up_sel[j]
    for p in range(1, 4):
        relay(p + 1)
        finish_inner(p)
    for p in range(5, count):
        relay(p)

    for copy in local[count:]:
        copy.wait()
    for k in others:
        hid_copy(k).wait_recv()
    for p in phases[0]:
        finish_end(p)
    low_parts(0)
    for k in (1, 2):
        spread(cache_in, *kv_args, 0, k).start()
    for j in range(requests):
        spread(up_sel, *up_args, j, 1 + j).wait_recv()
        pass_on(*up_args, j).start()
    for k in (1, 2):
        spread(cache_in, *kv_args, 1, k).start()
    finish_inner(4)

    low_q = low_of(0)
    for j in range(requests):
        spread(up_sel, *up_args, j, 2 - j).wait_recv()
        pass_on(*up_args, j).wait_recv()
    delta_q = jnp.dot(low_q, up_cols(0, q_width), preferred_element_type=jnp.float32)
    for j in range(requests):
        for h in range(head_count):
            cols = slice(h * head_dim, (h + 1) * head_dim)
            u = q_base[j, :, cols].astype(jnp.float32) + delta_q[j * rows : (j + 1) * rows, cols]
            queries[j, h * rows : (h + 1) * rows, :] = rotated(u).astype(jnp.bfloat16)
    for j in range(requests):
        spread(cache_in, *kv_args, j, 1 + j).wait_recv()
        pass_on(*kv_args, j).start()
    finish_inner(5)
    spread(cache_in, *kv_args, 0, 2).wait_recv()
    pass_on(*kv_args, 0).wait_recv()
    for g in groups:
        cached(0, g)
    finish_inner(6)
    for p in phases[1]:
        finish_end(p)
    low_parts(1)
    spread(cache_in, *kv_args, 1, 1).wait_recv()
    pass_on(*kv_args, 1).wait_recv()
    cached(1, 0)
    finish_inner(7)
    for g in groups[1:]:
        cached(1, g)

    low_k = low_of(1)
    delta_k = jnp.dot(low_k, up_cols(q_width, head_dim), preferred_element_type=jnp.float32)
    for j in range(requests):
        at = slice(j * rows, (j + 1) * rows)
        key = rotated(kv_base[j, :, :head_dim].astype(jnp.float32) + delta_k[at]).astype(jnp.bfloat16)
        new_kv[j, :, :head_dim] = key
        key_new[j, pl.ds(pl.multiple_of(seq * rows, rows), rows), :] = key
    for k in others:
        new_copy(0, k).start()
    for k in others:
        new_copy(0, k).wait_recv()
    token = lax.rem(lax.broadcasted_iota(jnp.int32, (group, span), 0), rows) + seq * rows
    visible = lax.broadcasted_iota(jnp.int32, (group, span), 1) <= token
    for j in range(requests):
        for g in groups:
            at = slice(g * group, (g + 1) * group)
            scores = (
                lax.dot_general(
                    queries[j, at, :], key_new[j], contract, preferred_element_type=jnp.float32
                )
                * scale
            )
            scores = jnp.where(visible, scores, masked_score)
            old = top[j, at, :]
            m = jnp.maximum(old, jnp.max(scores, axis=1, keepdims=True))
            w = jnp.exp2(scores - m[:, :1])
            factor = jnp.exp2(old - m)
            denom = total[j, at, :] * factor + jnp.sum(w, axis=1, keepdims=True)
            total[j, at, :] = denom
            acc[j, at, :] = acc[j, at, :] * factor
            fresh[j, at, :] = w.astype(jnp.bfloat16)

    for p in phases[2]:
        finish_end(p)
    low_parts(2)
    low_v = low_of(2)
    delta_v = jnp.dot(low_v, up_cols(q_width + head_dim, head_dim), preferred_element_type=jnp.float32)
    for j in range(requests):
        at = slice(j * rows, (j + 1) * rows)
        value = (kv_base[j, :, head_dim:].astype(jnp.float32) + delta_v[at]).astype(jnp.bfloat16)
        new_kv[j, :, head_dim:] = value
        value_new[j, pl.ds(pl.multiple_of(seq * rows, rows), rows), :] = value
    for k in others:
        new_copy(1, k).start()
    for k in others:
        new_copy(1, k).wait_recv()
    for j in range(requests):
        mixed = acc[j] + jnp.dot(fresh[j], value_new[j], preferred_element_type=jnp.float32)
        mixed = (mixed / total[j]).astype(jnp.bfloat16)
        attention = jnp.concatenate(
            [mixed[h * rows : (h + 1) * rows] for h in range(head_count)], axis=1
        )
        attn_out[j] = attention
        o_low[j] = lax.dot_general(
            attention,
            up_got[j, :, q_width + 2 * head_dim :],
            contract,
            preferred_element_type=jnp.float32,
        )

    for k in others:
        hid_copy(k).wait_send()
        for phase in range(3):
            part_copy(phase, k).wait_send()
        for kind in range(2):
            new_copy(kind, k).wait_send()
    for j in range(requests):
        for src, args in ((cache_in, kv_args), (up_sel, up_args)):
            for k in (1, 2):
                spread(src, *args, j, k).wait_send()
            pass_on(*args, j).wait_send()
    for p in range(count):
        across(p, 0, own[p]).wait_send()

        @pl.when(at_end)
        def _(p=p):
            z_copy(0, p, 0, to_first, own[p]).wait_send()
            if p == 0:
                for chip in range(1, 4):
                    across(p, chip).wait_send()

        @pl.when(inner)
        def _(p=p):
            z_copy(1, p, 0, to_second, own[p]).wait_send()
            z_copy(2, p, 1, to_second).wait_send()
            for chip in range(1, 4):
                across(p, chip).wait_send()
            if p == 0:
                z_copy(3, p, 0, to_first, own[p]).wait_send()
                z_copy(4, p, 2, to_first).wait_send()
                z_copy(5, p, 3, to_first).wait_send()
            else:
                z_sel(p, to_first).wait_send()


def fused(
    hidden_in, q_base, kv_base, cache_kv, req_adapter, slot_of_adapter, down_panels, up_panels
):
    requests, rows, _ = hidden_in.shape
    head_dim = kv_base.shape[2] // 2
    q_width = q_base.shape[2]
    pre_rows = cache_kv.shape[1]
    seq_count = lax.axis_size("seq")
    req_count = lax.axis_size("req")
    depth = down_panels.shape[1]
    rank_rows, up_width = up_panels.shape[1:]
    half_dim = head_dim // 2
    panel = down_panels[0].T
    positions = (
        pre_rows * seq_count
        + lax.axis_index("seq") * rows
        + jnp.arange(rows, dtype=jnp.int32)
    )
    inverse = 500000.0 ** (-jnp.arange(half_dim, dtype=jnp.float32) / half_dim)
    angles = positions.astype(jnp.float32)[:, None] * inverse[None, :]
    cosine = jnp.cos(angles)
    sine = jnp.sin(angles)
    cosine = jnp.concatenate([cosine, cosine], axis=1)
    sine = jnp.concatenate([-sine, sine], axis=1)
    span = seq_count * rows
    q_rows = q_width // head_dim * rows
    bf16, f32 = jnp.bfloat16, jnp.float32
    dma = pltpu.SemaphoreType.DMA
    smem = pl.BlockSpec(memory_space=pltpu.SMEM)
    vmem = pl.BlockSpec(memory_space=pltpu.VMEM)
    anywhere = pl.BlockSpec(memory_space=pltpu.HBM)
    half, quarter = half_dim // 2, half_dim // 4
    chunks = (half, half, half, half, half, quarter, quarter)
    phases = ((1, 2), (3, 4), (5, 6, 7))
    count = len(chunks) + 1
    shapes = [(rank_rows, up_width)] + [(n, depth) for n in chunks]
    return pl.pallas_call(
        functools.partial(attend_kernel, chunks, phases),
        out_shape=(
            jax.ShapeDtypeStruct((requests, rows, q_width), bf16),
            jax.ShapeDtypeStruct((requests, rows, half_dim), f32),
            jax.ShapeDtypeStruct((requests, rows, 2 * head_dim), bf16),
        ),
        in_specs=[smem, smem, anywhere, anywhere, anywhere, anywhere, vmem, vmem, vmem, vmem],
        out_specs=(vmem, vmem, vmem),
        scratch_shapes=[
            pltpu.VMEM((seq_count, requests, rows, depth), bf16),
            pltpu.VMEM((requests, rank_rows, up_width), bf16),
            pltpu.VMEM((requests, half_dim, up_width), bf16),
            pltpu.VMEM((requests, seq_count * pre_rows, 2 * head_dim), bf16),
            pltpu.VMEM((requests, span, head_dim), bf16),
            pltpu.VMEM((requests, span, head_dim), bf16),
            pltpu.VMEM((3, seq_count, rows, head_dim), f32),
            pltpu.VMEM((3, seq_count, rows, head_dim), f32),
            pltpu.VMEM((requests, q_rows, head_dim), bf16),
            pltpu.VMEM((requests, q_rows, head_dim), f32),
            pltpu.VMEM((requests, q_rows, head_dim), f32),
            pltpu.VMEM((requests, q_rows, head_dim), f32),
            pltpu.VMEM((requests, q_rows, span), bf16),
            dma((count + 2,)),
        ]
        + [dma((6, count))] * 2
        + [dma((4, count))] * 2
        + [dma((seq_count,))] * 2
        + [dma((requests, seq_count))] * 4
        + [dma((3, seq_count))] * 2
        + [dma((2, seq_count))] * 2
        + [pltpu.VMEM((req_count,) + shape, bf16) for shape in shapes]
        + [pltpu.VMEM((requests,) + shape, bf16) for shape in shapes[1:]],
        compiler_params=pltpu.CompilerParams(
            collective_id=0, has_side_effects=True, vmem_limit_bytes=48 * 1024 * 1024
        ),
    )(
        *[
            pltpu.with_memory_space_constraint(a, pltpu.HBM)
            for a in (
                req_adapter,
                slot_of_adapter,
                hidden_in,
                panel,
                up_panels[0],
                cache_kv,
                q_base,
                kv_base,
            )
        ],
        cosine,
        sine,
    )


def fits(mesh, hidden_in, down_panels):
    return (
        mesh.shape["req"] == 8
        and mesh.shape["seq"] == 4
        and hidden_in.shape[0] == 2
        and down_panels.shape[0] == 1
        and down_panels.shape[2] == 192
    )


def solution(mesh):
    def body(*arrays):
        return (fused if fits(mesh, arrays[0], arrays[6]) else on_device)(*arrays)

    return jax.shard_map(
        body,
        mesh=mesh,
        in_specs=(
            P("req", "seq", None),
            P("req", "seq", None),
            P("req", "seq", None),
            P("req", "seq", None),
            P(),
            P(),
            P("req", "seq", None),
            P("req", "seq", None),
        ),
        out_specs=(P("req", "seq", None), P("req", "seq", None), P("req", "seq", None)),
        check_vma=False,
    )
```

```python
import functools

import jax
import jax.numpy as jnp
from jax import lax
from jax.experimental import pallas as pl
from jax.experimental.pallas import tpu as pltpu
from jax.sharding import PartitionSpec as P

masked_score = -1e30
MESH = pl.DeviceIdType.MESH


def rotate(vectors, positions):
    half_dim = vectors.shape[-1] // 2
    inverse = 500000.0 ** (-jnp.arange(half_dim, dtype=jnp.float32) / half_dim)
    angles = positions.astype(jnp.float32)[:, None] * inverse[None, :]
    cosine = jnp.cos(angles)[:, None, :]
    sine_part = jnp.sin(angles)[:, None, :]
    first_half = vectors[..., :half_dim]
    second_half = vectors[..., half_dim:]
    return jnp.concatenate(
        [
            first_half * cosine - second_half * sine_part,
            second_half * cosine + first_half * sine_part,
        ],
        axis=-1,
    )


def on_device(
    hidden_in, q_base, kv_base, cache_kv, req_adapter, slot_of_adapter, down_panels, up_panels
):
    requests, seg_rows, model_width = hidden_in.shape
    head_dim = kv_base.shape[2] // 2
    q_width = q_base.shape[2]
    head_count = q_width // head_dim
    rank_all = down_panels.shape[2]
    rank_size = rank_all // 3
    pre_rows = cache_kv.shape[1]
    seq_count = lax.axis_size("seq")
    seq_pos = lax.axis_index("seq")
    req_pos = lax.axis_index("req")
    context = pre_rows * seq_count
    my_adapters = lax.dynamic_slice_in_dim(req_adapter, req_pos * requests, requests)
    wanted = jnp.take(slot_of_adapter, my_adapters)
    pieces = (
        lax.all_gather(down_panels, "req", axis=0, tiled=True),
        lax.all_gather(up_panels, "req", axis=0, tiled=True),
    )
    slot_ids = jnp.arange(pieces[0].shape[0], dtype=jnp.int32)
    onehot = (wanted[:, None] == slot_ids[None, :]).astype(jnp.bfloat16)
    down_part = jnp.einsum("js,snc->jnc", onehot, pieces[0], preferred_element_type=jnp.float32)
    up_part = jnp.einsum("js,snc->jnc", onehot, pieces[1], preferred_element_type=jnp.float32)
    down_sel = down_part
    up_sel = up_part
    down_sel = down_sel.astype(jnp.bfloat16)
    up_sel = up_sel.astype(jnp.bfloat16)
    up_full = lax.all_gather(up_sel, "seq", axis=1, tiled=True)
    low_rank = jnp.einsum(
        "jtd,jdc->jtc",
        hidden_in,
        lax.all_gather(down_sel, "seq", axis=1, tiled=True),
        preferred_element_type=jnp.float32,
    )
    low_half = low_rank.astype(jnp.bfloat16)
    delta_q = jnp.einsum(
        "jtr,jrc->jtc",
        low_half[:, :, :rank_size],
        up_full[:, :, :q_width],
        preferred_element_type=jnp.float32,
    )
    delta_k = jnp.einsum(
        "jtr,jrc->jtc",
        low_half[:, :, rank_size : 2 * rank_size],
        up_full[:, :, q_width : q_width + head_dim],
        preferred_element_type=jnp.float32,
    )
    delta_v = jnp.einsum(
        "jtr,jrc->jtc",
        low_half[:, :, 2 * rank_size :],
        up_full[:, :, q_width + head_dim : q_width + 2 * head_dim],
        preferred_element_type=jnp.float32,
    )
    query_index = seq_pos * seg_rows + jnp.arange(seg_rows, dtype=jnp.int32)
    positions = context + query_index
    queries = rotate(
        (q_base.astype(jnp.float32) + delta_q).reshape(requests, seg_rows, head_count, head_dim),
        positions,
    ).astype(jnp.bfloat16)
    keys_new = rotate(
        (kv_base[:, :, :head_dim].astype(jnp.float32) + delta_k)[:, :, None, :], positions
    )[:, :, 0, :]
    values_new = kv_base[:, :, head_dim:].astype(jnp.float32) + delta_v
    new_kv = jnp.concatenate([keys_new, values_new], axis=2).astype(jnp.bfloat16)
    local_kv = jnp.concatenate([cache_kv, new_kv], axis=1)
    kv_rows = pre_rows + seg_rows
    score_scale = head_dim ** (-0.5)

    def attend_block(state_now, key_block, first_row):
        running_max, running_sum, weighted = state_now
        key_part = key_block[:, :, :head_dim]
        value_part = key_block[:, :, head_dim:]
        scores = (
            jnp.einsum("jthd,jkd->jhtk", queries, key_part, preferred_element_type=jnp.float32)
            * score_scale
        )
        global_index = first_row + jnp.arange(key_block.shape[1], dtype=jnp.int32)
        owner_dev = global_index // kv_rows
        offset = global_index % kv_rows
        span_index = owner_dev * seg_rows + offset - pre_rows
        visible = (offset[None, :] < pre_rows) | (span_index[None, :] <= query_index[:, None])
        scores = jnp.where(visible[None, None], scores, masked_score)
        newest = jnp.maximum(running_max, jnp.max(scores, axis=-1))
        weights = jnp.where(visible[None, None], jnp.exp(scores - newest[..., None]), 0.0)
        factor = jnp.exp(running_max - newest)
        running_sum = running_sum * factor + jnp.sum(weights, axis=-1)
        weighted = weighted * factor[..., None] + jnp.einsum(
            "jhtk,jkd->jhtd",
            weights.astype(jnp.bfloat16),
            value_part,
            preferred_element_type=jnp.float32,
        )
        return (newest, running_sum, weighted)

    start_state = (
        jnp.full((requests, head_count, seg_rows), masked_score, jnp.float32),
        jnp.zeros((requests, head_count, seg_rows), jnp.float32),
        jnp.zeros((requests, head_count, seg_rows, head_dim), jnp.float32),
    )
    kv_piece = lax.all_gather(local_kv, "seq", axis=1, tiled=True)
    piece_rows = kv_piece.shape[1]

    def advance(block_number, state_inner):
        key_block = lax.dynamic_slice_in_dim(kv_piece, block_number * kv_rows, kv_rows, 1)
        return attend_block(state_inner, key_block, block_number * kv_rows)

    running_max, running_sum, weighted = lax.fori_loop(
        0, piece_rows // kv_rows, advance, start_state
    )
    mixed = weighted / running_sum[..., None]
    attn_out = (
        jnp.transpose(mixed, (0, 2, 1, 3)).reshape(requests, seg_rows, q_width).astype(jnp.bfloat16)
    )
    o_low = jnp.einsum(
        "jtc,jrc->jtr",
        attn_out,
        up_full[:, :, q_width + 2 * head_dim :],
        preferred_element_type=jnp.float32,
    )
    return (attn_out, o_low, new_kv)

def attend_kernel(
    pieces,
    phases,
    req_adapter,
    slot_of_adapter,
    hidden_in,
    down_in,
    up_in,
    cache_in,
    q_base,
    kv_base,
    cos_in,
    sin_in,
    attn_out,
    o_low,
    new_kv,
    hid,
    up_sel,
    up_got,
    out_sel,
    out_got,
    kv_all,
    key_new,
    value_new,
    part,
    part_got,
    queries,
    acc,
    top,
    total,
    fresh,
    local_sem,
    z_send,
    z_recv,
    mate_send,
    mate_recv,
    hid_send,
    hid_recv,
    kv_send,
    kv_recv,
    up_send,
    up_recv,
    out_send,
    out_recv,
    part_send,
    part_recv,
    new_send,
    new_recv,
    *panels,
):
    requests, rows, _ = q_base.shape
    seq_count, _, _, depth = hid.shape
    head_dim = kv_base.shape[2] // 2
    q_width = q_base.shape[2]
    head_count = q_width // head_dim
    rank = head_dim // 2
    pre_rows = cache_in.shape[1]
    up_rows = up_in.shape[0]
    span = seq_count * rows
    count = len(pieces)
    bufs, stages = panels[:count], panels[count:]
    up_piece, out_piece = [p for p in range(count) if pieces[p][0] == "up"]
    seq = lax.axis_index("seq")
    req = lax.axis_index("req")
    z = req // 2
    core = req % 2
    at_end = (z == 0) | (z == 3)
    inner = jnp.logical_not(at_end)
    left = z < 2
    first = jnp.where(z == 0, 1, jnp.where(z == 1, 0, jnp.where(z == 2, 3, 2)))
    second = jnp.where(at_end, 3 - first, 3 - z)
    third = jnp.where(at_end, 3 - z, 3 - first)
    chips = (z, first, second, third)
    slots = [chip * 2 + core for chip in chips]
    land = jnp.where(left, 2, 0)
    mate = {"req": z * 2 + (1 - core)}
    to_first = {"req": slots[1]}
    to_second = {"req": slots[2]}
    peers = [seq, seq + 1 - 2 * (seq % 2), (seq + 2) % 4, 3 - seq]
    others = range(1, seq_count)

    def send(src, dst, s_sem, r_sem, target):
        return pltpu.make_async_remote_copy(
            src_ref=src,
            dst_ref=dst,
            send_sem=s_sem,
            recv_sem=r_sem,
            device_id=target,
            device_id_type=MESH,
        )

    own = [
        up_in.at[:, pl.ds(begin, size)] if kind == "up" else down_in.at[pl.ds(begin, size)]
        for kind, begin, size in pieces
    ]
    local = [pltpu.make_async_copy(own[p], bufs[p].at[slots[0]], local_sem.at[p]) for p in range(count)]
    local.append(
        pltpu.make_async_copy(
            hidden_in.at[:, :, pl.ds(seq * depth, depth)], hid.at[seq], local_sem.at[count]
        )
    )
    local.append(
        pltpu.make_async_copy(
            cache_in, kv_all.at[:, pl.ds(seq * pre_rows, pre_rows), :], local_sem.at[count + 1]
        )
    )

    barrier = pltpu.get_barrier_semaphore()
    for k in others:
        pl.semaphore_signal(barrier, inc=1, device_id={"seq": peers[k]}, device_id_type=MESH)
    pl.semaphore_signal(barrier, inc=1, device_id=mate, device_id_type=MESH)
    pl.semaphore_signal(barrier, inc=1, device_id=to_first, device_id_type=MESH)

    @pl.when(inner)
    def _():
        pl.semaphore_signal(barrier, inc=1, device_id=to_second, device_id_type=MESH)

    for copy in local:
        copy.start()
    pl.semaphore_wait(barrier, seq_count + 1 + inner.astype(jnp.int32))

    def z_copy(kind, p, chip, target, src=None):
        here = bufs[p].at[slots[chip]]
        return send(here if src is None else src, here, z_send.at[kind, p], z_recv.at[kind, p], target)

    def z_sel(p, target):
        return send(
            stages[p], bufs[p].at[pl.ds(land, requests)], z_send.at[3, p], z_recv.at[3, p], target
        )

    def across(p, chip, src=None):
        here = bufs[p].at[slots[chip]]
        return send(
            here if src is None else src, here, mate_send.at[chip, p], mate_recv.at[chip, p], mate
        )

    def hid_copy(k):
        return send(
            hidden_in.at[:, :, pl.ds(peers[k] * depth, depth)],
            hid.at[seq],
            hid_send.at[k],
            hid_recv.at[k],
            {"seq": peers[k]},
        )

    def spread(src, dst, size, sems, j, k):
        at = pl.ds(pl.multiple_of(seq * size, size), size)
        return send(src.at[j], dst.at[j, at], sems[0].at[j, k], sems[1].at[j, k], {"seq": peers[k]})

    def pass_on(dst, size, sems, j):
        here = dst.at[j, pl.ds(pl.multiple_of(peers[1 + j] * size, size), size)]
        return send(here, here, sems[0].at[j, 3], sems[1].at[j, 3], {"seq": peers[2 - j]})

    kv_args = (kv_all, pre_rows, (kv_send, kv_recv))
    up_args = (up_got, up_rows, (up_send, up_recv))
    out_args = (out_got, up_rows, (out_send, out_recv))

    def part_copy(phase, k):
        return send(
            part.at[phase, peers[k]],
            part_got.at[phase, k],
            part_send.at[phase, k],
            part_recv.at[phase, k],
            {"seq": peers[k]},
        )

    def new_copy(kind, k):
        ref = (key_new, value_new)[kind]
        here = ref.at[:, pl.ds(pl.multiple_of(seq * rows, rows), rows), :]
        return send(here, here, new_send.at[kind, k], new_recv.at[kind, k], {"seq": peers[k]})

    @pl.when(at_end)
    def _():
        for p in range(count):
            z_copy(0, p, 0, to_first, own[p]).start()

    @pl.when(inner)
    def _():
        z_copy(1, 0, 0, to_second, own[0]).start()
        z_copy(3, up_piece, 0, to_first, own[up_piece]).start()
        z_copy(1, 1, 0, to_second, own[1]).start()

    for k in others:
        hid_copy(k).start()
    for p in range(count):
        across(p, 0, own[p]).start()

    wanted = [slot_of_adapter[req_adapter[req * requests + j]] for j in range(requests)]
    mine = [
        jnp.where(at_end & (w // 2 != z), land + j, w) for j, w in enumerate(wanted)
    ]

    def relay(p):
        @pl.when(inner)
        def _():
            z_copy(0, p, 1, to_first).wait_recv()
            z_copy(2, p, 1, to_second).start()
            across(p, 1).start()
            ahead = 2 if p == 0 else p + 1
            if p != 1 and ahead < count:
                z_copy(1, ahead, 0, to_second, own[ahead]).start()

    def from_second(p):
        @pl.when(inner)
        def _():
            z_copy(1, p, 2, to_second).wait_recv()
            across(p, 2).start()
            if p == up_piece:
                z_copy(4, p, 2, to_first).start()

    def from_third(p):
        @pl.when(inner)
        def _():
            z_copy(2, p, 3, to_second).wait_recv()
            across(p, 3).start()
            if p == up_piece:
                z_copy(5, p, 3, to_first).start()
            local[p].wait()
            for chip in range(4):
                across(p, chip).wait_recv()
            if p != up_piece:
                for j in range(requests):
                    w = slot_of_adapter[req_adapter[slots[1] * requests + j]]
                    w = jnp.where(w // 2 == first, slots[0], w)
                    stages[p][j] = bufs[p][w]
                z_sel(p, to_first).start()

    def finish_inner(p):
        from_second(p)
        from_third(p)

    def finish_end(p):
        @pl.when(at_end)
        def _():
            if p == up_piece:
                for kind in range(3):
                    z_copy(3 + kind, p, 1 + kind, to_first).wait_recv()
                    across(p, 1 + kind).start()
            else:
                z_sel(p, to_first).wait_recv()
            local[p].wait()
            for chip in range(4 if p == up_piece else 1):
                across(p, chip).wait_recv()

    contract = (((1,), (1,)), ((), ()))

    def low_parts(phase):
        thin = []
        for j in range(requests):
            panel = jnp.concatenate([bufs[p][mine[j]] for p in phases[phase]], axis=0)
            h = hid[:, j].reshape(span, depth)
            thin.append(lax.dot_general(h, panel, contract, preferred_element_type=jnp.float32))
        joined = jnp.concatenate(thin, axis=1)
        for s in range(seq_count):
            part[phase, s] = joined[s * rows : (s + 1) * rows]
        for k in others:
            part_copy(phase, k).start()

    def low_of(phase):
        for k in others:
            part_copy(phase, k).wait_recv()
        low = part[phase, seq]
        for k in others:
            low = low + part_got[phase, k]
        low = jnp.concatenate([low] * requests, axis=0)
        row = lax.broadcasted_iota(jnp.int32, low.shape, 0) // rows
        lane = lax.broadcasted_iota(jnp.int32, low.shape, 1) // rank
        return jnp.where(row == lane, low, 0.0).astype(jnp.bfloat16)

    def up_cols(begin, size):
        return up_got[:, :, begin : begin + size].reshape(requests * rank, size)

    cosine = cos_in[...]
    sine = sin_in[...]

    def rotated(u):
        return u * cosine + pltpu.roll(u, rank, 1) * sine

    scale = head_dim ** (-0.5) * 1.4426950408889634
    group = 4 * rows
    groups = range(head_count * rows // group)

    def cached(j, g):
        at = slice(g * group, (g + 1) * group)
        scores = (
            lax.dot_general(
                queries[j, at, :], kv_all[j, :, :head_dim], contract, preferred_element_type=jnp.float32
            )
            * scale
        )
        m = jnp.max(scores, axis=1, keepdims=True)
        w = jnp.exp2(scores - m)
        top[j, at, :] = jnp.broadcast_to(m, (group, head_dim))
        total[j, at, :] = jnp.broadcast_to(jnp.sum(w, axis=1, keepdims=True), (group, head_dim))
        acc[j, at, :] = jnp.dot(
            w.astype(jnp.bfloat16), kv_all[j, :, head_dim:], preferred_element_type=jnp.float32
        )

    relay(0)
    relay(1)
    from_second(up_piece)
    finish_inner(0)
    from_third(up_piece)
    finish_end(up_piece)
    for j in range(requests):
        up_sel[j] = bufs[up_piece][wanted[j]]
    for j in range(requests):
        for k in (1, 2):
            spread(up_sel, *up_args, j, k).start()
        up_got[j, pl.ds(pl.multiple_of(seq * up_rows, up_rows), up_rows)] = up_sel[j]
    for k in (1, 2):
        spread(cache_in, *kv_args, 0, k).start()
    relay(2)
    for p in range(2, 7):
        relay(p + 1)
        finish_inner(p)
    for p in range(8, count):
        relay(p)

    for copy in local[count:]:
        copy.wait()
    for k in others:
        hid_copy(k).wait_recv()
    for p in phases[0]:
        finish_end(p)
    low_parts(0)
    for j in range(requests):
        spread(up_sel, *up_args, j, 1 + j).wait_recv()
        pass_on(*up_args, j).start()
    for k in (1, 2):
        spread(cache_in, *kv_args, 1, k).start()
    finish_inner(7)
    finish_inner(8)
    spread(cache_in, *kv_args, 0, 1).wait_recv()
    pass_on(*kv_args, 0).start()

    low_q = low_of(0)
    for j in range(requests):
        spread(up_sel, *up_args, j, 2 - j).wait_recv()
        pass_on(*up_args, j).wait_recv()
    delta_q = jnp.dot(low_q, up_cols(0, q_width), preferred_element_type=jnp.float32)
    for j in range(requests):
        for h in range(head_count):
            cols = slice(h * head_dim, (h + 1) * head_dim)
            u = q_base[j, :, cols].astype(jnp.float32) + delta_q[j * rows : (j + 1) * rows, cols]
            queries[j, h * rows : (h + 1) * rows, :] = rotated(u).astype(jnp.bfloat16)
    finish_inner(9)
    for p in phases[1]:
        finish_end(p)
    low_parts(1)
    spread(cache_in, *kv_args, 1, 2).wait_recv()
    pass_on(*kv_args, 1).start()
    finish_inner(10)
    spread(cache_in, *kv_args, 0, 2).wait_recv()
    pass_on(*kv_args, 0).wait_recv()
    for g in groups:
        cached(0, g)
    finish_inner(11)

    low_k = low_of(1)
    delta_k = jnp.dot(low_k, up_cols(q_width, head_dim), preferred_element_type=jnp.float32)
    for j in range(requests):
        at = slice(j * rows, (j + 1) * rows)
        key = rotated(kv_base[j, :, :head_dim].astype(jnp.float32) + delta_k[at]).astype(jnp.bfloat16)
        new_kv[j, :, :head_dim] = key
        key_new[j, pl.ds(pl.multiple_of(seq * rows, rows), rows), :] = key
    for k in others:
        new_copy(0, k).start()
    spread(cache_in, *kv_args, 1, 1).wait_recv()
    pass_on(*kv_args, 1).wait_recv()
    for g in groups:
        cached(1, g)
    finish_inner(12)
    for k in others:
        new_copy(0, k).wait_recv()
    token = lax.rem(lax.broadcasted_iota(jnp.int32, (group, span), 0), rows) + seq * rows
    visible = lax.broadcasted_iota(jnp.int32, (group, span), 1) <= token

    def in_span(j):
        for g in groups:
            at = slice(g * group, (g + 1) * group)
            scores = (
                lax.dot_general(
                    queries[j, at, :], key_new[j], contract, preferred_element_type=jnp.float32
                )
                * scale
            )
            scores = jnp.where(visible, scores, masked_score)
            old = top[j, at, :]
            m = jnp.maximum(old, jnp.max(scores, axis=1, keepdims=True))
            w = jnp.exp2(scores - m[:, :1])
            factor = jnp.exp2(old - m)
            denom = total[j, at, :] * factor + jnp.sum(w, axis=1, keepdims=True)
            total[j, at, :] = denom
            acc[j, at, :] = acc[j, at, :] * factor
            fresh[j, at, :] = w.astype(jnp.bfloat16)

    in_span(0)
    finish_inner(out_piece)
    in_span(1)
    for p in phases[2]:
        finish_end(p)
    low_parts(2)
    finish_end(out_piece)
    for j in range(requests):
        out_sel[j] = bufs[out_piece][mine[j]]
    for j in range(requests):
        for k in (1, 2):
            spread(out_sel, *out_args, j, k).start()
        out_got[j, pl.ds(pl.multiple_of(seq * up_rows, up_rows), up_rows)] = out_sel[j]
    low_v = low_of(2)
    delta_v = jnp.dot(low_v, up_cols(q_width + head_dim, head_dim), preferred_element_type=jnp.float32)
    for j in range(requests):
        at = slice(j * rows, (j + 1) * rows)
        value = (kv_base[j, :, head_dim:].astype(jnp.float32) + delta_v[at]).astype(jnp.bfloat16)
        new_kv[j, :, head_dim:] = value
        value_new[j, pl.ds(pl.multiple_of(seq * rows, rows), rows), :] = value
    for k in others:
        new_copy(1, k).start()
    for j in range(requests):
        spread(out_sel, *out_args, j, 1 + j).wait_recv()
        pass_on(*out_args, j).start()
    for k in others:
        new_copy(1, k).wait_recv()
    for j in range(requests):
        mixed = acc[j] + jnp.dot(fresh[j], value_new[j], preferred_element_type=jnp.float32)
        mixed = (mixed / total[j]).astype(jnp.bfloat16)
        for h in range(head_count):
            attn_out[j, :, h * head_dim : (h + 1) * head_dim] = mixed[h * rows : (h + 1) * rows]
    for j in range(requests):
        spread(out_sel, *out_args, j, 2 - j).wait_recv()
        pass_on(*out_args, j).wait_recv()
    for j in range(requests):
        o_low[j] = lax.dot_general(
            attn_out[j], out_got[j], contract, preferred_element_type=jnp.float32
        )

    for k in others:
        hid_copy(k).wait_send()
        for phase in range(3):
            part_copy(phase, k).wait_send()
        for kind in range(2):
            new_copy(kind, k).wait_send()
    for j in range(requests):
        for src, args in ((cache_in, kv_args), (up_sel, up_args), (out_sel, out_args)):
            for k in (1, 2):
                spread(src, *args, j, k).wait_send()
            pass_on(*args, j).wait_send()
    for p in range(count):
        across(p, 0, own[p]).wait_send()

        @pl.when(at_end)
        def _(p=p):
            z_copy(0, p, 0, to_first, own[p]).wait_send()
            if p == up_piece:
                for chip in range(1, 4):
                    across(p, chip).wait_send()

        @pl.when(inner)
        def _(p=p):
            z_copy(1, p, 0, to_second, own[p]).wait_send()
            z_copy(2, p, 1, to_second).wait_send()
            for chip in range(1, 4):
                across(p, chip).wait_send()
            if p == up_piece:
                z_copy(3, p, 0, to_first, own[p]).wait_send()
                z_copy(4, p, 2, to_first).wait_send()
                z_copy(5, p, 3, to_first).wait_send()
            else:
                z_sel(p, to_first).wait_send()


def fused(
    hidden_in, q_base, kv_base, cache_kv, req_adapter, slot_of_adapter, down_panels, up_panels
):
    requests, rows, _ = hidden_in.shape
    head_dim = kv_base.shape[2] // 2
    q_width = q_base.shape[2]
    pre_rows = cache_kv.shape[1]
    seq_count = lax.axis_size("seq")
    req_count = lax.axis_size("req")
    depth = down_panels.shape[1]
    rank_rows, up_width = up_panels.shape[1:]
    half_dim = head_dim // 2
    panel = down_panels[0].T
    positions = (
        pre_rows * seq_count
        + lax.axis_index("seq") * rows
        + jnp.arange(rows, dtype=jnp.int32)
    )
    inverse = 500000.0 ** (-jnp.arange(half_dim, dtype=jnp.float32) / half_dim)
    angles = positions.astype(jnp.float32)[:, None] * inverse[None, :]
    cosine = jnp.cos(angles)
    sine = jnp.sin(angles)
    cosine = jnp.concatenate([cosine, cosine], axis=1)
    sine = jnp.concatenate([-sine, sine], axis=1)
    span = seq_count * rows
    q_rows = q_width // head_dim * rows
    bf16, f32 = jnp.bfloat16, jnp.float32
    dma = pltpu.SemaphoreType.DMA
    smem = pl.BlockSpec(memory_space=pltpu.SMEM)
    vmem = pl.BlockSpec(memory_space=pltpu.VMEM)
    anywhere = pl.BlockSpec(memory_space=pltpu.HBM)
    t = half_dim // 4
    up_part = q_width + 2 * head_dim
    pieces = [("down", i * t, t) for i in range(12)]
    pieces.insert(1, ("up", 0, up_part))
    pieces.append(("up", up_part, up_width - up_part))
    phases = ((0, 2, 3, 4), (5, 6, 7, 8), (9, 10, 11, 12))
    count = len(pieces)
    shapes = [(rank_rows, n) if kind == "up" else (n, depth) for kind, _, n in pieces]
    return pl.pallas_call(
        functools.partial(attend_kernel, pieces, phases),
        out_shape=(
            jax.ShapeDtypeStruct((requests, rows, q_width), bf16),
            jax.ShapeDtypeStruct((requests, rows, half_dim), f32),
            jax.ShapeDtypeStruct((requests, rows, 2 * head_dim), bf16),
        ),
        in_specs=[smem, smem, anywhere, anywhere, anywhere, anywhere, vmem, vmem, vmem, vmem],
        out_specs=(vmem, vmem, vmem),
        scratch_shapes=[
            pltpu.VMEM((seq_count, requests, rows, depth), bf16),
            pltpu.VMEM((requests, rank_rows, up_part), bf16),
            pltpu.VMEM((requests, half_dim, up_part), bf16),
            pltpu.VMEM((requests, rank_rows, up_width - up_part), bf16),
            pltpu.VMEM((requests, half_dim, up_width - up_part), bf16),
            pltpu.VMEM((requests, seq_count * pre_rows, 2 * head_dim), bf16),
            pltpu.VMEM((requests, span, head_dim), bf16),
            pltpu.VMEM((requests, span, head_dim), bf16),
            pltpu.VMEM((3, seq_count, rows, head_dim), f32),
            pltpu.VMEM((3, seq_count, rows, head_dim), f32),
            pltpu.VMEM((requests, q_rows, head_dim), bf16),
            pltpu.VMEM((requests, q_rows, head_dim), f32),
            pltpu.VMEM((requests, q_rows, head_dim), f32),
            pltpu.VMEM((requests, q_rows, head_dim), f32),
            pltpu.VMEM((requests, q_rows, span), bf16),
            dma((count + 2,)),
        ]
        + [dma((6, count))] * 2
        + [dma((4, count))] * 2
        + [dma((seq_count,))] * 2
        + [dma((requests, seq_count))] * 6
        + [dma((3, seq_count))] * 2
        + [dma((2, seq_count))] * 2
        + [pltpu.VMEM((req_count,) + shape, bf16) for shape in shapes]
        + [pltpu.VMEM((requests,) + shape, bf16) for shape in shapes],
        compiler_params=pltpu.CompilerParams(
            collective_id=0, has_side_effects=True, vmem_limit_bytes=48 * 1024 * 1024
        ),
    )(
        *[
            pltpu.with_memory_space_constraint(a, pltpu.HBM)
            for a in (
                req_adapter,
                slot_of_adapter,
                hidden_in,
                panel,
                up_panels[0],
                cache_kv,
                q_base,
                kv_base,
            )
        ],
        cosine,
        sine,
    )


def fits(mesh, hidden_in, down_panels):
    return (
        mesh.shape["req"] == 8
        and mesh.shape["seq"] == 4
        and hidden_in.shape[0] == 2
        and down_panels.shape[0] == 1
        and down_panels.shape[2] == 192
    )


def solution(mesh):
    def body(*arrays):
        return (fused if fits(mesh, arrays[0], arrays[6]) else on_device)(*arrays)

    return jax.shard_map(
        body,
        mesh=mesh,
        in_specs=(
            P("req", "seq", None),
            P("req", "seq", None),
            P("req", "seq", None),
            P("req", "seq", None),
            P(),
            P(),
            P("req", "seq", None),
            P("req", "seq", None),
        ),
        out_specs=(P("req", "seq", None), P("req", "seq", None), P("req", "seq", None)),
        check_vma=False,
    )
```

```python
import functools

import jax
import jax.numpy as jnp
from jax import lax
from jax.experimental import pallas as pl
from jax.experimental.pallas import tpu as pltpu
from jax.sharding import PartitionSpec as P

masked_score = -1e30
MESH = pl.DeviceIdType.MESH


def rotate(vectors, positions):
    half_dim = vectors.shape[-1] // 2
    inverse = 500000.0 ** (-jnp.arange(half_dim, dtype=jnp.float32) / half_dim)
    angles = positions.astype(jnp.float32)[:, None] * inverse[None, :]
    cosine = jnp.cos(angles)[:, None, :]
    sine_part = jnp.sin(angles)[:, None, :]
    first_half = vectors[..., :half_dim]
    second_half = vectors[..., half_dim:]
    return jnp.concatenate(
        [
            first_half * cosine - second_half * sine_part,
            second_half * cosine + first_half * sine_part,
        ],
        axis=-1,
    )


def on_device(
    hidden_in, q_base, kv_base, cache_kv, req_adapter, slot_of_adapter, down_panels, up_panels
):
    requests, seg_rows, model_width = hidden_in.shape
    head_dim = kv_base.shape[2] // 2
    q_width = q_base.shape[2]
    head_count = q_width // head_dim
    rank_all = down_panels.shape[2]
    rank_size = rank_all // 3
    pre_rows = cache_kv.shape[1]
    seq_count = lax.axis_size("seq")
    seq_pos = lax.axis_index("seq")
    req_pos = lax.axis_index("req")
    context = pre_rows * seq_count
    my_adapters = lax.dynamic_slice_in_dim(req_adapter, req_pos * requests, requests)
    wanted = jnp.take(slot_of_adapter, my_adapters)
    pieces = (
        lax.all_gather(down_panels, "req", axis=0, tiled=True),
        lax.all_gather(up_panels, "req", axis=0, tiled=True),
    )
    slot_ids = jnp.arange(pieces[0].shape[0], dtype=jnp.int32)
    onehot = (wanted[:, None] == slot_ids[None, :]).astype(jnp.bfloat16)
    down_part = jnp.einsum("js,snc->jnc", onehot, pieces[0], preferred_element_type=jnp.float32)
    up_part = jnp.einsum("js,snc->jnc", onehot, pieces[1], preferred_element_type=jnp.float32)
    down_sel = down_part
    up_sel = up_part
    down_sel = down_sel.astype(jnp.bfloat16)
    up_sel = up_sel.astype(jnp.bfloat16)
    up_full = lax.all_gather(up_sel, "seq", axis=1, tiled=True)
    low_rank = jnp.einsum(
        "jtd,jdc->jtc",
        hidden_in,
        lax.all_gather(down_sel, "seq", axis=1, tiled=True),
        preferred_element_type=jnp.float32,
    )
    low_half = low_rank.astype(jnp.bfloat16)
    delta_q = jnp.einsum(
        "jtr,jrc->jtc",
        low_half[:, :, :rank_size],
        up_full[:, :, :q_width],
        preferred_element_type=jnp.float32,
    )
    delta_k = jnp.einsum(
        "jtr,jrc->jtc",
        low_half[:, :, rank_size : 2 * rank_size],
        up_full[:, :, q_width : q_width + head_dim],
        preferred_element_type=jnp.float32,
    )
    delta_v = jnp.einsum(
        "jtr,jrc->jtc",
        low_half[:, :, 2 * rank_size :],
        up_full[:, :, q_width + head_dim : q_width + 2 * head_dim],
        preferred_element_type=jnp.float32,
    )
    query_index = seq_pos * seg_rows + jnp.arange(seg_rows, dtype=jnp.int32)
    positions = context + query_index
    queries = rotate(
        (q_base.astype(jnp.float32) + delta_q).reshape(requests, seg_rows, head_count, head_dim),
        positions,
    ).astype(jnp.bfloat16)
    keys_new = rotate(
        (kv_base[:, :, :head_dim].astype(jnp.float32) + delta_k)[:, :, None, :], positions
    )[:, :, 0, :]
    values_new = kv_base[:, :, head_dim:].astype(jnp.float32) + delta_v
    new_kv = jnp.concatenate([keys_new, values_new], axis=2).astype(jnp.bfloat16)
    local_kv = jnp.concatenate([cache_kv, new_kv], axis=1)
    kv_rows = pre_rows + seg_rows
    score_scale = head_dim ** (-0.5)

    def attend_block(state_now, key_block, first_row):
        running_max, running_sum, weighted = state_now
        key_part = key_block[:, :, :head_dim]
        value_part = key_block[:, :, head_dim:]
        scores = (
            jnp.einsum("jthd,jkd->jhtk", queries, key_part, preferred_element_type=jnp.float32)
            * score_scale
        )
        global_index = first_row + jnp.arange(key_block.shape[1], dtype=jnp.int32)
        owner_dev = global_index // kv_rows
        offset = global_index % kv_rows
        span_index = owner_dev * seg_rows + offset - pre_rows
        visible = (offset[None, :] < pre_rows) | (span_index[None, :] <= query_index[:, None])
        scores = jnp.where(visible[None, None], scores, masked_score)
        newest = jnp.maximum(running_max, jnp.max(scores, axis=-1))
        weights = jnp.where(visible[None, None], jnp.exp(scores - newest[..., None]), 0.0)
        factor = jnp.exp(running_max - newest)
        running_sum = running_sum * factor + jnp.sum(weights, axis=-1)
        weighted = weighted * factor[..., None] + jnp.einsum(
            "jhtk,jkd->jhtd",
            weights.astype(jnp.bfloat16),
            value_part,
            preferred_element_type=jnp.float32,
        )
        return (newest, running_sum, weighted)

    start_state = (
        jnp.full((requests, head_count, seg_rows), masked_score, jnp.float32),
        jnp.zeros((requests, head_count, seg_rows), jnp.float32),
        jnp.zeros((requests, head_count, seg_rows, head_dim), jnp.float32),
    )
    kv_piece = lax.all_gather(local_kv, "seq", axis=1, tiled=True)
    piece_rows = kv_piece.shape[1]

    def advance(block_number, state_inner):
        key_block = lax.dynamic_slice_in_dim(kv_piece, block_number * kv_rows, kv_rows, 1)
        return attend_block(state_inner, key_block, block_number * kv_rows)

    running_max, running_sum, weighted = lax.fori_loop(
        0, piece_rows // kv_rows, advance, start_state
    )
    mixed = weighted / running_sum[..., None]
    attn_out = (
        jnp.transpose(mixed, (0, 2, 1, 3)).reshape(requests, seg_rows, q_width).astype(jnp.bfloat16)
    )
    o_low = jnp.einsum(
        "jtc,jrc->jtr",
        attn_out,
        up_full[:, :, q_width + 2 * head_dim :],
        preferred_element_type=jnp.float32,
    )
    return (attn_out, o_low, new_kv)

def attend_kernel(
    pieces,
    phases,
    req_adapter,
    slot_of_adapter,
    hidden_in,
    down_in,
    up_in,
    cache_in,
    q_in,
    kv_in,
    cos_in,
    sin_in,
    attn_out,
    o_low,
    new_kv,
    q_base,
    kv_base,
    hid,
    up_sel,
    up_got,
    out_sel,
    out_got,
    kv_all,
    key_new,
    value_new,
    part,
    part_got,
    base_all,
    low_all,
    last_all,
    queries,
    acc,
    top,
    total,
    fresh,
    local_sem,
    z_send,
    z_recv,
    mate_send,
    mate_recv,
    hid_send,
    hid_recv,
    kv_send,
    kv_recv,
    up_send,
    up_recv,
    out_send,
    out_recv,
    part_send,
    part_recv,
    new_send,
    new_recv,
    base_send,
    base_recv,
    low_send,
    low_recv,
    last_send,
    last_recv,
    *panels,
):
    requests, rows, _ = q_base.shape
    seq_count, _, _, depth = hid.shape
    head_dim = kv_base.shape[2] // 2
    q_width = q_base.shape[2]
    head_count = q_width // head_dim
    rank = head_dim // 2
    pre_rows = cache_in.shape[1]
    up_rows = up_in.shape[0]
    span = seq_count * rows
    count = len(pieces)
    bufs, stages = panels[:count], panels[count:]
    up_piece, out_piece = [p for p in range(count) if pieces[p][0] == "up"]
    whole = (0, up_piece)
    seq = lax.axis_index("seq")
    req = lax.axis_index("req")
    z = req // 2
    core = req % 2
    at_end = (z == 0) | (z == 3)
    inner = jnp.logical_not(at_end)
    left = z < 2
    first = jnp.where(z == 0, 1, jnp.where(z == 1, 0, jnp.where(z == 2, 3, 2)))
    second = jnp.where(at_end, 3 - first, 3 - z)
    third = jnp.where(at_end, 3 - z, 3 - first)
    chips = (z, first, second, third)
    slots = [chip * 2 + core for chip in chips]
    land = jnp.where(left, 2, 0)
    mate = {"req": z * 2 + (1 - core)}
    to_first = {"req": slots[1]}
    to_second = {"req": slots[2]}
    peers = [seq, seq + 1 - 2 * (seq % 2), (seq + 2) % 4, 3 - seq]
    others = range(1, seq_count)

    def send(src, dst, s_sem, r_sem, target):
        return pltpu.make_async_remote_copy(
            src_ref=src,
            dst_ref=dst,
            send_sem=s_sem,
            recv_sem=r_sem,
            device_id=target,
            device_id_type=MESH,
        )

    own = [
        up_in.at[:, pl.ds(begin, size)] if kind == "up" else down_in.at[pl.ds(begin, size)]
        for kind, begin, size in pieces
    ]
    local = [pltpu.make_async_copy(own[p], bufs[p].at[slots[0]], local_sem.at[p]) for p in range(count)]
    local.append(
        pltpu.make_async_copy(
            hidden_in.at[:, :, pl.ds(seq * depth, depth)], hid.at[seq], local_sem.at[count]
        )
    )
    local.append(
        pltpu.make_async_copy(
            cache_in, kv_all.at[:, pl.ds(seq * pre_rows, pre_rows), :], local_sem.at[count + 1]
        )
    )

    local.append(
        pltpu.make_async_copy(
            kv_in.at[:, :, pl.ds(head_dim, head_dim)],
            base_all.at[:, pl.ds(pl.multiple_of(seq * rows, rows), rows), :],
            local_sem.at[count + 4],
        )
    )
    local.append(pltpu.make_async_copy(q_in, q_base, local_sem.at[count + 2]))
    local.append(pltpu.make_async_copy(kv_in, kv_base, local_sem.at[count + 3]))

    barrier = pltpu.get_barrier_semaphore()
    for k in others:
        pl.semaphore_signal(barrier, inc=1, device_id={"seq": peers[k]}, device_id_type=MESH)
    pl.semaphore_signal(barrier, inc=1, device_id=mate, device_id_type=MESH)
    pl.semaphore_signal(barrier, inc=1, device_id=to_first, device_id_type=MESH)

    @pl.when(inner)
    def _():
        pl.semaphore_signal(barrier, inc=1, device_id=to_second, device_id_type=MESH)

    pl.semaphore_wait(barrier, seq_count + 1 + inner.astype(jnp.int32))

    def z_copy(kind, p, chip, target, src=None):
        here = bufs[p].at[slots[chip]]
        return send(here if src is None else src, here, z_send.at[kind, p], z_recv.at[kind, p], target)

    def z_sel(p, target):
        return send(
            stages[p], bufs[p].at[pl.ds(land, requests)], z_send.at[3, p], z_recv.at[3, p], target
        )

    def across(p, chip, src=None):
        here = bufs[p].at[slots[chip]]
        return send(
            here if src is None else src, here, mate_send.at[chip, p], mate_recv.at[chip, p], mate
        )

    def hid_copy(k):
        return send(
            hidden_in.at[:, :, pl.ds(peers[k] * depth, depth)],
            hid.at[seq],
            hid_send.at[k],
            hid_recv.at[k],
            {"seq": peers[k]},
        )

    def spread(src, dst, size, sems, j, k):
        at = pl.ds(pl.multiple_of(seq * size, size), size)
        return send(src.at[j], dst.at[j, at], sems[0].at[j, k], sems[1].at[j, k], {"seq": peers[k]})

    def pass_on(dst, size, sems, j):
        here = dst.at[j, pl.ds(pl.multiple_of(peers[1 + j] * size, size), size)]
        return send(here, here, sems[0].at[j, 3], sems[1].at[j, 3], {"seq": peers[2 - j]})

    kv_args = (kv_all, pre_rows, (kv_send, kv_recv))
    up_args = (up_got, up_rows, (up_send, up_recv))
    out_args = (out_got, up_rows, (out_send, out_recv))

    def part_copy(phase, k):
        return send(
            part.at[phase, peers[k]],
            part_got.at[phase, k],
            part_send.at[phase, k],
            part_recv.at[phase, k],
            {"seq": peers[k]},
        )

    def new_copy(k):
        here = key_new.at[:, pl.ds(pl.multiple_of(seq * rows, rows), rows), :]
        return send(here, here, new_send.at[k], new_recv.at[k], {"seq": peers[k]})

    def base_copy(k):
        return send(
            kv_in.at[:, :, pl.ds(head_dim, head_dim)],
            base_all.at[:, pl.ds(pl.multiple_of(seq * rows, rows), rows), :],
            base_send.at[k],
            base_recv.at[k],
            {"seq": peers[k]},
        )

    def low_copy(k):
        here = low_all.at[pl.ds(pl.multiple_of(seq * rows, rows), rows)]
        return send(here, here, low_send.at[k], low_recv.at[k], {"seq": peers[k]})

    def last_copy(k):
        here = last_all.at[seq]
        return send(here, here, last_send.at[k], last_recv.at[k], {"seq": peers[k]})

    @pl.when(at_end)
    def _():
        for p in range(2):
            z_copy(0, p, 0, to_first, own[p]).start()

    @pl.when(inner)
    def _():
        for p in range(3):
            z_copy(1, p, 0, to_second, own[p]).start()
            if p in whole:
                z_copy(3, p, 0, to_first, own[p]).start()

    for k in others:
        hid_copy(k).start()

    @pl.when(at_end)
    def _():
        for p in range(2, count):
            z_copy(0, p, 0, to_first, own[p]).start()

    for copy in local:
        copy.start()
    for p in range(count):
        across(p, 0, own[p]).start()

    wanted = [slot_of_adapter[req_adapter[req * requests + j]] for j in range(requests)]
    mine = [
        jnp.where(at_end & (w // 2 != z), land + j, w) for j, w in enumerate(wanted)
    ]

    def relay(p):
        @pl.when(inner)
        def _():
            z_copy(0, p, 1, to_first).wait_recv()
            z_copy(2, p, 1, to_second).start()
            across(p, 1).start()
            ahead = 3 if p == 0 else p + 2
            if p != 1 and ahead < count:
                z_copy(1, ahead, 0, to_second, own[ahead]).start()

    def from_second(p):
        @pl.when(inner)
        def _():
            z_copy(1, p, 2, to_second).wait_recv()
            across(p, 2).start()
            if p in whole:
                z_copy(4, p, 2, to_first).start()

    def from_third(p):
        @pl.when(inner)
        def _():
            z_copy(2, p, 3, to_second).wait_recv()
            across(p, 3).start()
            if p in whole:
                z_copy(5, p, 3, to_first).start()
            local[p].wait()
            for chip in range(4):
                across(p, chip).wait_recv()
            if p not in whole:
                for j in range(requests):
                    w = slot_of_adapter[req_adapter[slots[1] * requests + j]]
                    w = jnp.where(w // 2 == first, slots[0], w)
                    stages[p][j] = bufs[p][w]
                z_sel(p, to_first).start()

    def finish_inner(p):
        from_second(p)
        from_third(p)

    def finish_end(p):
        @pl.when(at_end)
        def _():
            if p in whole:
                for kind in range(3):
                    z_copy(3 + kind, p, 1 + kind, to_first).wait_recv()
                    across(p, 1 + kind).start()
            else:
                z_sel(p, to_first).wait_recv()
            local[p].wait()
            for chip in range(4 if p in whole else 1):
                across(p, chip).wait_recv()

    contract = (((1,), (1,)), ((), ()))

    def low_parts(phase):
        thin = []
        for j in range(requests):
            panel = [bufs[p][wanted[j] if p in whole else mine[j]] for p in phases[phase]]
            short = rank - sum(pieces[p][2] for p in phases[phase])
            if short:
                panel.append(jnp.zeros((short, depth), jnp.bfloat16))
            panel = jnp.concatenate(panel, axis=0)
            h = hid[:, j].reshape(span, depth)
            thin.append(lax.dot_general(h, panel, contract, preferred_element_type=jnp.float32))
        joined = jnp.concatenate(thin, axis=1)
        for s in range(seq_count):
            part[phase, s] = joined[s * rows : (s + 1) * rows]
        for k in others:
            part_copy(phase, k).start()

    def low_sum(phase):
        for k in others:
            part_copy(phase, k).wait_recv()
        low = part[phase, seq]
        for k in others:
            low = low + part_got[phase, k]
        return low

    def stacked(low):
        size, width = low.shape
        low = jnp.concatenate([low] * requests, axis=0)
        row = lax.broadcasted_iota(jnp.int32, low.shape, 0) // size
        lane = lax.broadcasted_iota(jnp.int32, low.shape, 1) // (width // requests)
        return jnp.where(row == lane, low, 0.0).astype(jnp.bfloat16)

    def low_of(phase):
        return stacked(low_sum(phase))

    def up_cols(begin, size):
        return up_got[:, :, begin : begin + size].reshape(requests * rank, size)

    cosine = cos_in[...]
    sine = sin_in[...]

    def rotated(u):
        return u * cosine + pltpu.roll(u, rank, 1) * sine

    scale = head_dim ** (-0.5) * 1.4426950408889634
    group = 4 * rows
    groups = range(head_count * rows // group)

    def cached(j, g):
        at = slice(g * group, (g + 1) * group)
        scores = (
            lax.dot_general(
                queries[j, at, :], kv_all[j, :, :head_dim], contract, preferred_element_type=jnp.float32
            )
            * scale
        )
        m = jnp.max(scores, axis=1, keepdims=True)
        w = jnp.exp2(scores - m)
        top[j, at, :] = jnp.broadcast_to(m, (group, head_dim))
        total[j, at, :] = jnp.broadcast_to(jnp.sum(w, axis=1, keepdims=True), (group, head_dim))
        acc[j, at, :] = jnp.dot(
            w.astype(jnp.bfloat16), kv_all[j, :, head_dim:], preferred_element_type=jnp.float32
        )

    relay(0)
    from_second(0)
    relay(1)
    from_second(1)
    relay(2)
    from_third(0)
    relay(3)
    from_third(1)
    relay(4)
    finish_inner(2)
    finish_end(0)
    finish_end(1)
    for j in range(requests):
        up_sel[j] = bufs[up_piece][wanted[j]]
    for j in range(requests):
        for k in (1, 2):
            spread(up_sel, *up_args, j, k).start()
        up_got[j, pl.ds(pl.multiple_of(seq * up_rows, up_rows), up_rows)] = up_sel[j]
    for k in (1, 2):
        spread(cache_in, *kv_args, 0, k).start()
    for p in range(3, 7):
        relay(p + 2)
        finish_inner(p)
    for p in range(9, count):
        relay(p)

    for copy in local[count:]:
        copy.wait()
    for k in others:
        hid_copy(k).wait_recv()
    finish_inner(7)
    for p in phases[0][1:]:
        finish_end(p)
    low_parts(0)
    for j in range(requests):
        spread(up_sel, *up_args, j, 1 + j).wait_recv()
        pass_on(*up_args, j).start()
    for k in (1, 2):
        spread(cache_in, *kv_args, 1, k).start()
    for k in others:
        base_copy(k).start()
    finish_inner(8)
    spread(cache_in, *kv_args, 0, 1).wait_recv()
    pass_on(*kv_args, 0).start()

    finish_inner(out_piece)
    finish_inner(10)
    low_q = low_of(0)
    for j in range(requests):
        spread(up_sel, *up_args, j, 2 - j).wait_recv()
        pass_on(*up_args, j).wait_recv()
    delta_q = jnp.dot(low_q, up_cols(0, q_width), preferred_element_type=jnp.float32)
    for j in range(requests):
        for h in range(head_count):
            cols = slice(h * head_dim, (h + 1) * head_dim)
            u = q_base[j, :, cols].astype(jnp.float32) + delta_q[j * rows : (j + 1) * rows, cols]
            queries[j, h * rows : (h + 1) * rows, :] = rotated(u).astype(jnp.bfloat16)
    for p in phases[1]:
        finish_end(p)
    low_parts(1)
    spread(cache_in, *kv_args, 1, 2).wait_recv()
    pass_on(*kv_args, 1).start()
    finish_end(out_piece)
    for j in range(requests):
        out_sel[j] = bufs[out_piece][mine[j]]
    for j in range(requests):
        for k in (1, 2):
            spread(out_sel, *out_args, j, k).start()
        out_got[j, pl.ds(pl.multiple_of(seq * up_rows, up_rows), up_rows)] = out_sel[j]
    finish_inner(11)
    finish_inner(12)
    spread(cache_in, *kv_args, 0, 2).wait_recv()
    pass_on(*kv_args, 0).wait_recv()
    for g in groups:
        cached(0, g)

    low_k = low_of(1)
    delta_k = jnp.dot(low_k, up_cols(q_width, head_dim), preferred_element_type=jnp.float32)
    for j in range(requests):
        at = slice(j * rows, (j + 1) * rows)
        key = rotated(kv_base[j, :, :head_dim].astype(jnp.float32) + delta_k[at]).astype(jnp.bfloat16)
        new_kv[j, :, :head_dim] = key
        key_new[j, pl.ds(pl.multiple_of(seq * rows, rows), rows), :] = key
    for k in others:
        new_copy(k).start()
    finish_inner(13)
    spread(cache_in, *kv_args, 1, 1).wait_recv()
    pass_on(*kv_args, 1).wait_recv()
    for g in groups:
        cached(1, g)
    for j in range(requests):
        spread(out_sel, *out_args, j, 1 + j).wait_recv()
        pass_on(*out_args, j).start()
    for p in phases[2]:
        finish_end(p)
    low_parts(2)
    for k in others:
        new_copy(k).wait_recv()
    token = lax.rem(lax.broadcasted_iota(jnp.int32, (group, span), 0), rows) + seq * rows
    visible = lax.broadcasted_iota(jnp.int32, (group, span), 1) <= token

    def in_span(j):
        for g in groups:
            at = slice(g * group, (g + 1) * group)
            scores = (
                lax.dot_general(
                    queries[j, at, :], key_new[j], contract, preferred_element_type=jnp.float32
                )
                * scale
            )
            scores = jnp.where(visible, scores, masked_score)
            old = top[j, at, :]
            m = jnp.maximum(old, jnp.max(scores, axis=1, keepdims=True))
            w = jnp.exp2(scores - m[:, :1])
            factor = jnp.exp2(old - m)
            denom = total[j, at, :] * factor + jnp.sum(w, axis=1, keepdims=True)
            total[j, at, :] = denom
            acc[j, at, :] = acc[j, at, :] * factor
            fresh[j, at, :] = w.astype(jnp.bfloat16)

    in_span(0)
    in_span(1)
    last = count - 1
    finish_end(last)
    tail = pieces[last][2]
    for j in range(requests):
        h = hid[:, j].reshape(span, depth)
        last_all[seq, j * tail : (j + 1) * tail, :] = lax.dot_general(
            bufs[last][mine[j]], h, contract, preferred_element_type=jnp.float32
        )
    for k in others:
        last_copy(k).start()
    low_all[pl.ds(pl.multiple_of(seq * rows, rows), rows), :] = low_sum(2).astype(jnp.bfloat16)
    for k in others:
        low_copy(k).start()
    for k in others:
        base_copy(k).wait_recv()
    up_v = up_cols(q_width + head_dim, head_dim)
    for k in others:
        last_copy(k).wait_recv()
    low_last = last_all[0]
    for s in range(1, seq_count):
        low_last = low_last + last_all[s]
    up_last = jnp.concatenate(
        [up_v[(j + 1) * rank - tail : (j + 1) * rank] for j in range(requests)], axis=0
    )
    delta_last = jnp.dot(stacked(low_last.T), up_last, preferred_element_type=jnp.float32)
    for k in others:
        low_copy(k).wait_recv()
    low_v = stacked(low_all[...].astype(jnp.float32))
    delta_v = jnp.dot(low_v, up_v, preferred_element_type=jnp.float32) + delta_last
    for j in range(requests):
        value = base_all[j].astype(jnp.float32) + delta_v[j * span : (j + 1) * span]
        value_new[j] = value.astype(jnp.bfloat16)
    for j in range(requests):
        mixed = acc[j] + jnp.dot(fresh[j], value_new[j], preferred_element_type=jnp.float32)
        mixed = (mixed / total[j]).astype(jnp.bfloat16)
        for h in range(head_count):
            attn_out[j, :, h * head_dim : (h + 1) * head_dim] = mixed[h * rows : (h + 1) * rows]
        new_kv[j, :, head_dim:] = value_new[j, pl.ds(pl.multiple_of(seq * rows, rows), rows), :]
    for j in range(requests):
        spread(out_sel, *out_args, j, 2 - j).wait_recv()
        pass_on(*out_args, j).wait_recv()
    for j in range(requests):
        o_low[j] = lax.dot_general(
            attn_out[j], out_got[j], contract, preferred_element_type=jnp.float32
        )

    for k in others:
        hid_copy(k).wait_send()
        for phase in range(3):
            part_copy(phase, k).wait_send()
        for copy in (new_copy, base_copy, low_copy, last_copy):
            copy(k).wait_send()
    for j in range(requests):
        for src, args in ((cache_in, kv_args), (up_sel, up_args), (out_sel, out_args)):
            for k in (1, 2):
                spread(src, *args, j, k).wait_send()
            pass_on(*args, j).wait_send()
    for p in range(count):
        across(p, 0, own[p]).wait_send()

        @pl.when(at_end)
        def _(p=p):
            z_copy(0, p, 0, to_first, own[p]).wait_send()
            if p in whole:
                for chip in range(1, 4):
                    across(p, chip).wait_send()

        @pl.when(inner)
        def _(p=p):
            z_copy(1, p, 0, to_second, own[p]).wait_send()
            z_copy(2, p, 1, to_second).wait_send()
            for chip in range(1, 4):
                across(p, chip).wait_send()
            if p in whole:
                z_copy(3, p, 0, to_first, own[p]).wait_send()
                z_copy(4, p, 2, to_first).wait_send()
                z_copy(5, p, 3, to_first).wait_send()
            else:
                z_sel(p, to_first).wait_send()


def fused(
    hidden_in, q_base, kv_base, cache_kv, req_adapter, slot_of_adapter, down_panels, up_panels
):
    requests, rows, _ = hidden_in.shape
    head_dim = kv_base.shape[2] // 2
    q_width = q_base.shape[2]
    pre_rows = cache_kv.shape[1]
    seq_count = lax.axis_size("seq")
    req_count = lax.axis_size("req")
    depth = down_panels.shape[1]
    rank_rows, up_width = up_panels.shape[1:]
    half_dim = head_dim // 2
    panel = down_panels[0].T
    positions = (
        pre_rows * seq_count
        + lax.axis_index("seq") * rows
        + jnp.arange(rows, dtype=jnp.int32)
    )
    inverse = 500000.0 ** (-jnp.arange(half_dim, dtype=jnp.float32) / half_dim)
    angles = positions.astype(jnp.float32)[:, None] * inverse[None, :]
    cosine = jnp.cos(angles)
    sine = jnp.sin(angles)
    cosine = jnp.concatenate([cosine, cosine], axis=1)
    sine = jnp.concatenate([-sine, sine], axis=1)
    span = seq_count * rows
    q_rows = q_width // head_dim * rows
    bf16, f32 = jnp.bfloat16, jnp.float32
    dma = pltpu.SemaphoreType.DMA
    smem = pl.BlockSpec(memory_space=pltpu.SMEM)
    vmem = pl.BlockSpec(memory_space=pltpu.VMEM)
    anywhere = pl.BlockSpec(memory_space=pltpu.HBM)
    t = half_dim // 4
    up_part = q_width + 2 * head_dim
    pieces = [("down", i * t, t) for i in range(12)]
    pieces.insert(1, ("up", 0, up_part))
    pieces.insert(9, ("up", up_part, up_width - up_part))
    phases = ((0, 2, 3, 4), (5, 6, 7, 8), (10, 11, 12))
    count = len(pieces)
    shapes = [(rank_rows, n) if kind == "up" else (n, depth) for kind, _, n in pieces]
    return pl.pallas_call(
        functools.partial(attend_kernel, pieces, phases),
        out_shape=(
            jax.ShapeDtypeStruct((requests, rows, q_width), bf16),
            jax.ShapeDtypeStruct((requests, rows, half_dim), f32),
            jax.ShapeDtypeStruct((requests, rows, 2 * head_dim), bf16),
        ),
        in_specs=[smem, smem] + [anywhere] * 6 + [vmem, vmem],
        out_specs=(vmem, vmem, vmem),
        scratch_shapes=[
            pltpu.VMEM((requests, rows, q_width), bf16),
            pltpu.VMEM((requests, rows, 2 * head_dim), bf16),
            pltpu.VMEM((seq_count, requests, rows, depth), bf16),
            pltpu.VMEM((requests, rank_rows, up_part), bf16),
            pltpu.VMEM((requests, half_dim, up_part), bf16),
            pltpu.VMEM((requests, rank_rows, up_width - up_part), bf16),
            pltpu.VMEM((requests, half_dim, up_width - up_part), bf16),
            pltpu.VMEM((requests, seq_count * pre_rows, 2 * head_dim), bf16),
            pltpu.VMEM((requests, span, head_dim), bf16),
            pltpu.VMEM((requests, span, head_dim), bf16),
            pltpu.VMEM((3, seq_count, rows, head_dim), f32),
            pltpu.VMEM((3, seq_count, rows, head_dim), f32),
            pltpu.VMEM((requests, span, head_dim), bf16),
            pltpu.VMEM((span, head_dim), bf16),
            pltpu.VMEM((seq_count, requests * t, span), f32),
            pltpu.VMEM((requests, q_rows, head_dim), bf16),
            pltpu.VMEM((requests, q_rows, head_dim), f32),
            pltpu.VMEM((requests, q_rows, head_dim), f32),
            pltpu.VMEM((requests, q_rows, head_dim), f32),
            pltpu.VMEM((requests, q_rows, span), bf16),
            dma((count + 5,)),
        ]
        + [dma((6, count))] * 2
        + [dma((4, count))] * 2
        + [dma((seq_count,))] * 2
        + [dma((requests, seq_count))] * 6
        + [dma((3, seq_count))] * 2
        + [dma((seq_count,))] * 8
        + [pltpu.VMEM((req_count,) + shape, bf16) for shape in shapes]
        + [pltpu.VMEM((requests,) + shape, bf16) for shape in shapes],
        compiler_params=pltpu.CompilerParams(
            collective_id=0, has_side_effects=True, vmem_limit_bytes=48 * 1024 * 1024
        ),
    )(
        *[
            pltpu.with_memory_space_constraint(a, pltpu.HBM)
            for a in (
                req_adapter,
                slot_of_adapter,
                hidden_in,
                panel,
                up_panels[0],
                cache_kv,
                q_base,
                kv_base,
            )
        ],
        cosine,
        sine,
    )


def fits(mesh, hidden_in, down_panels):
    return (
        mesh.shape["req"] == 8
        and mesh.shape["seq"] == 4
        and hidden_in.shape[0] == 2
        and down_panels.shape[0] == 1
        and down_panels.shape[2] == 192
    )


def solution(mesh):
    def body(*arrays):
        return (fused if fits(mesh, arrays[0], arrays[6]) else on_device)(*arrays)

    return jax.shard_map(
        body,
        mesh=mesh,
        in_specs=(
            P("req", "seq", None),
            P("req", "seq", None),
            P("req", "seq", None),
            P("req", "seq", None),
            P(),
            P(),
            P("req", "seq", None),
            P("req", "seq", None),
        ),
        out_specs=(P("req", "seq", None), P("req", "seq", None), P("req", "seq", None)),
        check_vma=False,
    )
```

```python
import functools

import jax
import jax.numpy as jnp
from jax import lax
from jax.experimental import pallas as pl
from jax.experimental.pallas import tpu as pltpu
from jax.sharding import PartitionSpec as P

masked_score = -1e30
MESH = pl.DeviceIdType.MESH


def rotate(vectors, positions):
    half_dim = vectors.shape[-1] // 2
    inverse = 500000.0 ** (-jnp.arange(half_dim, dtype=jnp.float32) / half_dim)
    angles = positions.astype(jnp.float32)[:, None] * inverse[None, :]
    cosine = jnp.cos(angles)[:, None, :]
    sine_part = jnp.sin(angles)[:, None, :]
    first_half = vectors[..., :half_dim]
    second_half = vectors[..., half_dim:]
    return jnp.concatenate(
        [
            first_half * cosine - second_half * sine_part,
            second_half * cosine + first_half * sine_part,
        ],
        axis=-1,
    )


def on_device(
    hidden_in, q_base, kv_base, cache_kv, req_adapter, slot_of_adapter, down_panels, up_panels
):
    requests, seg_rows, model_width = hidden_in.shape
    head_dim = kv_base.shape[2] // 2
    q_width = q_base.shape[2]
    head_count = q_width // head_dim
    rank_all = down_panels.shape[2]
    rank_size = rank_all // 3
    pre_rows = cache_kv.shape[1]
    seq_count = lax.axis_size("seq")
    seq_pos = lax.axis_index("seq")
    req_pos = lax.axis_index("req")
    context = pre_rows * seq_count
    my_adapters = lax.dynamic_slice_in_dim(req_adapter, req_pos * requests, requests)
    wanted = jnp.take(slot_of_adapter, my_adapters)
    pieces = (
        lax.all_gather(down_panels, "req", axis=0, tiled=True),
        lax.all_gather(up_panels, "req", axis=0, tiled=True),
    )
    slot_ids = jnp.arange(pieces[0].shape[0], dtype=jnp.int32)
    onehot = (wanted[:, None] == slot_ids[None, :]).astype(jnp.bfloat16)
    down_part = jnp.einsum("js,snc->jnc", onehot, pieces[0], preferred_element_type=jnp.float32)
    up_part = jnp.einsum("js,snc->jnc", onehot, pieces[1], preferred_element_type=jnp.float32)
    down_sel = down_part
    up_sel = up_part
    down_sel = down_sel.astype(jnp.bfloat16)
    up_sel = up_sel.astype(jnp.bfloat16)
    up_full = lax.all_gather(up_sel, "seq", axis=1, tiled=True)
    low_rank = jnp.einsum(
        "jtd,jdc->jtc",
        hidden_in,
        lax.all_gather(down_sel, "seq", axis=1, tiled=True),
        preferred_element_type=jnp.float32,
    )
    low_half = low_rank.astype(jnp.bfloat16)
    delta_q = jnp.einsum(
        "jtr,jrc->jtc",
        low_half[:, :, :rank_size],
        up_full[:, :, :q_width],
        preferred_element_type=jnp.float32,
    )
    delta_k = jnp.einsum(
        "jtr,jrc->jtc",
        low_half[:, :, rank_size : 2 * rank_size],
        up_full[:, :, q_width : q_width + head_dim],
        preferred_element_type=jnp.float32,
    )
    delta_v = jnp.einsum(
        "jtr,jrc->jtc",
        low_half[:, :, 2 * rank_size :],
        up_full[:, :, q_width + head_dim : q_width + 2 * head_dim],
        preferred_element_type=jnp.float32,
    )
    query_index = seq_pos * seg_rows + jnp.arange(seg_rows, dtype=jnp.int32)
    positions = context + query_index
    queries = rotate(
        (q_base.astype(jnp.float32) + delta_q).reshape(requests, seg_rows, head_count, head_dim),
        positions,
    ).astype(jnp.bfloat16)
    keys_new = rotate(
        (kv_base[:, :, :head_dim].astype(jnp.float32) + delta_k)[:, :, None, :], positions
    )[:, :, 0, :]
    values_new = kv_base[:, :, head_dim:].astype(jnp.float32) + delta_v
    new_kv = jnp.concatenate([keys_new, values_new], axis=2).astype(jnp.bfloat16)
    local_kv = jnp.concatenate([cache_kv, new_kv], axis=1)
    kv_rows = pre_rows + seg_rows
    score_scale = head_dim ** (-0.5)

    def attend_block(state_now, key_block, first_row):
        running_max, running_sum, weighted = state_now
        key_part = key_block[:, :, :head_dim]
        value_part = key_block[:, :, head_dim:]
        scores = (
            jnp.einsum("jthd,jkd->jhtk", queries, key_part, preferred_element_type=jnp.float32)
            * score_scale
        )
        global_index = first_row + jnp.arange(key_block.shape[1], dtype=jnp.int32)
        owner_dev = global_index // kv_rows
        offset = global_index % kv_rows
        span_index = owner_dev * seg_rows + offset - pre_rows
        visible = (offset[None, :] < pre_rows) | (span_index[None, :] <= query_index[:, None])
        scores = jnp.where(visible[None, None], scores, masked_score)
        newest = jnp.maximum(running_max, jnp.max(scores, axis=-1))
        weights = jnp.where(visible[None, None], jnp.exp(scores - newest[..., None]), 0.0)
        factor = jnp.exp(running_max - newest)
        running_sum = running_sum * factor + jnp.sum(weights, axis=-1)
        weighted = weighted * factor[..., None] + jnp.einsum(
            "jhtk,jkd->jhtd",
            weights.astype(jnp.bfloat16),
            value_part,
            preferred_element_type=jnp.float32,
        )
        return (newest, running_sum, weighted)

    start_state = (
        jnp.full((requests, head_count, seg_rows), masked_score, jnp.float32),
        jnp.zeros((requests, head_count, seg_rows), jnp.float32),
        jnp.zeros((requests, head_count, seg_rows, head_dim), jnp.float32),
    )
    kv_piece = lax.all_gather(local_kv, "seq", axis=1, tiled=True)
    piece_rows = kv_piece.shape[1]

    def advance(block_number, state_inner):
        key_block = lax.dynamic_slice_in_dim(kv_piece, block_number * kv_rows, kv_rows, 1)
        return attend_block(state_inner, key_block, block_number * kv_rows)

    running_max, running_sum, weighted = lax.fori_loop(
        0, piece_rows // kv_rows, advance, start_state
    )
    mixed = weighted / running_sum[..., None]
    attn_out = (
        jnp.transpose(mixed, (0, 2, 1, 3)).reshape(requests, seg_rows, q_width).astype(jnp.bfloat16)
    )
    o_low = jnp.einsum(
        "jtc,jrc->jtr",
        attn_out,
        up_full[:, :, q_width + 2 * head_dim :],
        preferred_element_type=jnp.float32,
    )
    return (attn_out, o_low, new_kv)

def attend_kernel(
    pieces,
    phases,
    req_adapter,
    slot_of_adapter,
    hidden_in,
    down_in,
    up_in,
    cache_in,
    q_in,
    kv_in,
    cos_in,
    sin_in,
    attn_out,
    o_low,
    new_kv,
    q_base,
    kv_base,
    hid,
    up_sel,
    up_got,
    out_sel,
    out_got,
    kv_all,
    key_new,
    value_new,
    part,
    part_got,
    base_all,
    low_all,
    last_all,
    queries,
    acc,
    top,
    total,
    fresh,
    local_sem,
    z_send,
    z_recv,
    mate_send,
    mate_recv,
    hid_send,
    hid_recv,
    kv_send,
    kv_recv,
    up_send,
    up_recv,
    out_send,
    out_recv,
    part_send,
    part_recv,
    new_send,
    new_recv,
    base_send,
    base_recv,
    low_send,
    low_recv,
    last_send,
    last_recv,
    *panels,
):
    requests, rows, _ = q_base.shape
    seq_count, _, _, depth = hid.shape
    head_dim = kv_base.shape[2] // 2
    q_width = q_base.shape[2]
    head_count = q_width // head_dim
    rank = head_dim // 2
    pre_rows = cache_in.shape[1]
    up_rows = up_in.shape[0]
    span = seq_count * rows
    count = len(pieces)
    bufs, stages = panels[:count], panels[count:]
    up_piece, out_piece = [p for p in range(count) if pieces[p][0] == "up"]
    whole = (0, up_piece)
    seq = lax.axis_index("seq")
    req = lax.axis_index("req")
    z = req // 2
    core = req % 2
    at_end = (z == 0) | (z == 3)
    inner = jnp.logical_not(at_end)
    left = z < 2
    first = jnp.where(z == 0, 1, jnp.where(z == 1, 0, jnp.where(z == 2, 3, 2)))
    second = jnp.where(at_end, 3 - first, 3 - z)
    third = jnp.where(at_end, 3 - z, 3 - first)
    chips = (z, first, second, third)
    slots = [chip * 2 + core for chip in chips]
    land = jnp.where(left, 2, 0)
    mate = {"req": z * 2 + (1 - core)}
    to_first = {"req": slots[1]}
    to_second = {"req": slots[2]}
    peers = [seq, seq + 1 - 2 * (seq % 2), (seq + 2) % 4, 3 - seq]
    others = range(1, seq_count)

    def send(src, dst, s_sem, r_sem, target):
        return pltpu.make_async_remote_copy(
            src_ref=src,
            dst_ref=dst,
            send_sem=s_sem,
            recv_sem=r_sem,
            device_id=target,
            device_id_type=MESH,
        )

    own = [
        up_in.at[:, pl.ds(begin, size)] if kind == "up" else down_in.at[pl.ds(begin, size)]
        for kind, begin, size in pieces
    ]
    local = [pltpu.make_async_copy(own[p], bufs[p].at[slots[0]], local_sem.at[p]) for p in range(count)]
    local.append(
        pltpu.make_async_copy(
            hidden_in.at[:, :, pl.ds(seq * depth, depth)], hid.at[seq], local_sem.at[count]
        )
    )
    local.append(
        pltpu.make_async_copy(
            cache_in, kv_all.at[:, pl.ds(seq * pre_rows, pre_rows), :], local_sem.at[count + 1]
        )
    )

    local.append(
        pltpu.make_async_copy(
            kv_in.at[:, :, pl.ds(head_dim, head_dim)],
            base_all.at[:, pl.ds(pl.multiple_of(seq * rows, rows), rows), :],
            local_sem.at[count + 4],
        )
    )
    local.append(pltpu.make_async_copy(q_in, q_base, local_sem.at[count + 2]))
    local.append(pltpu.make_async_copy(kv_in, kv_base, local_sem.at[count + 3]))

    barrier = pltpu.get_barrier_semaphore()
    for k in others:
        pl.semaphore_signal(barrier, inc=1, device_id={"seq": peers[k]}, device_id_type=MESH)
    pl.semaphore_signal(barrier, inc=1, device_id=mate, device_id_type=MESH)
    pl.semaphore_signal(barrier, inc=1, device_id=to_first, device_id_type=MESH)

    @pl.when(inner)
    def _():
        pl.semaphore_signal(barrier, inc=1, device_id=to_second, device_id_type=MESH)

    pl.semaphore_wait(barrier, seq_count + 1 + inner.astype(jnp.int32))

    def z_copy(kind, p, chip, target, src=None):
        here = bufs[p].at[slots[chip]]
        return send(here if src is None else src, here, z_send.at[kind, p], z_recv.at[kind, p], target)

    def z_sel(p, target):
        return send(
            stages[p], bufs[p].at[pl.ds(land, requests)], z_send.at[3, p], z_recv.at[3, p], target
        )

    def across(p, chip, src=None):
        here = bufs[p].at[slots[chip]]
        return send(
            here if src is None else src, here, mate_send.at[chip, p], mate_recv.at[chip, p], mate
        )

    def hid_copy(k):
        return send(
            hidden_in.at[:, :, pl.ds(peers[k] * depth, depth)],
            hid.at[seq],
            hid_send.at[k],
            hid_recv.at[k],
            {"seq": peers[k]},
        )

    def spread(src, dst, size, sems, j, k):
        at = pl.ds(pl.multiple_of(seq * size, size), size)
        return send(src.at[j], dst.at[j, at], sems[0].at[j, k], sems[1].at[j, k], {"seq": peers[k]})

    def pass_on(dst, size, sems, j):
        here = dst.at[j, pl.ds(pl.multiple_of(peers[1 + j] * size, size), size)]
        return send(here, here, sems[0].at[j, 3], sems[1].at[j, 3], {"seq": peers[2 - j]})

    kv_args = (kv_all, pre_rows, (kv_send, kv_recv))
    up_args = (up_got, up_rows, (up_send, up_recv))
    out_args = (out_got, up_rows, (out_send, out_recv))

    def part_copy(phase, k):
        return send(
            part.at[phase, peers[k]],
            part_got.at[phase, k],
            part_send.at[phase, k],
            part_recv.at[phase, k],
            {"seq": peers[k]},
        )

    def new_copy(k):
        here = key_new.at[:, pl.ds(pl.multiple_of(seq * rows, rows), rows), :]
        return send(here, here, new_send.at[k], new_recv.at[k], {"seq": peers[k]})

    def base_copy(k):
        return send(
            kv_in.at[:, :, pl.ds(head_dim, head_dim)],
            base_all.at[:, pl.ds(pl.multiple_of(seq * rows, rows), rows), :],
            base_send.at[k],
            base_recv.at[k],
            {"seq": peers[k]},
        )

    def low_copy(k):
        here = low_all.at[pl.ds(pl.multiple_of(seq * rows, rows), rows)]
        return send(here, here, low_send.at[k], low_recv.at[k], {"seq": peers[k]})

    def last_copy(k):
        here = last_all.at[seq]
        return send(here, here, last_send.at[k], last_recv.at[k], {"seq": peers[k]})

    @pl.when(at_end)
    def _():
        for p in range(2):
            z_copy(0, p, 0, to_first, own[p]).start()

    @pl.when(inner)
    def _():
        for p in range(3):
            z_copy(1, p, 0, to_second, own[p]).start()
            if p in whole:
                z_copy(3, p, 0, to_first, own[p]).start()

    for k in others:
        hid_copy(k).start()

    @pl.when(at_end)
    def _():
        for p in range(2, count):
            z_copy(0, p, 0, to_first, own[p]).start()

    for copy in local:
        copy.start()
    for p in range(count):
        across(p, 0, own[p]).start()

    wanted = [slot_of_adapter[req_adapter[req * requests + j]] for j in range(requests)]
    mine = [
        jnp.where(at_end & (w // 2 != z), land + j, w) for j, w in enumerate(wanted)
    ]

    def relay(p):
        @pl.when(inner)
        def _():
            z_copy(0, p, 1, to_first).wait_recv()
            z_copy(2, p, 1, to_second).start()
            across(p, 1).start()
            ahead = 3 if p == 0 else p + 2
            if p != 1 and ahead < count:
                z_copy(1, ahead, 0, to_second, own[ahead]).start()

    def from_second(p):
        @pl.when(inner)
        def _():
            z_copy(1, p, 2, to_second).wait_recv()
            across(p, 2).start()
            if p in whole:
                z_copy(4, p, 2, to_first).start()

    def from_third(p):
        @pl.when(inner)
        def _():
            z_copy(2, p, 3, to_second).wait_recv()
            across(p, 3).start()
            if p in whole:
                z_copy(5, p, 3, to_first).start()
            local[p].wait()
            for chip in range(4):
                across(p, chip).wait_recv()
            if p not in whole:
                for j in range(requests):
                    w = slot_of_adapter[req_adapter[slots[1] * requests + j]]
                    w = jnp.where(w // 2 == first, slots[0], w)
                    stages[p][j] = bufs[p][w]
                z_sel(p, to_first).start()

    def finish_inner(p):
        from_second(p)
        from_third(p)

    def finish_end(p):
        @pl.when(at_end)
        def _():
            if p in whole:
                for kind in range(3):
                    z_copy(3 + kind, p, 1 + kind, to_first).wait_recv()
                    across(p, 1 + kind).start()
            else:
                z_sel(p, to_first).wait_recv()
            local[p].wait()
            for chip in range(4 if p in whole else 1):
                across(p, chip).wait_recv()

    contract = (((1,), (1,)), ((), ()))

    def low_parts(phase):
        thin = []
        for j in range(requests):
            panel = [bufs[p][wanted[j] if p in whole else mine[j]] for p in phases[phase]]
            short = rank - sum(pieces[p][2] for p in phases[phase])
            if short:
                panel.append(jnp.zeros((short, depth), jnp.bfloat16))
            panel = jnp.concatenate(panel, axis=0)
            h = hid[:, j].reshape(span, depth)
            thin.append(lax.dot_general(h, panel, contract, preferred_element_type=jnp.float32))
        joined = jnp.concatenate(thin, axis=1)
        for s in range(seq_count):
            part[phase, s] = joined[s * rows : (s + 1) * rows]
        for k in others:
            part_copy(phase, k).start()

    def low_sum(phase):
        for k in others:
            part_copy(phase, k).wait_recv()
        low = part[phase, seq]
        for k in others:
            low = low + part_got[phase, k]
        return low

    def stacked(low):
        size, width = low.shape
        low = jnp.concatenate([low] * requests, axis=0)
        row = lax.broadcasted_iota(jnp.int32, low.shape, 0) // size
        lane = lax.broadcasted_iota(jnp.int32, low.shape, 1) // (width // requests)
        return jnp.where(row == lane, low, 0.0).astype(jnp.bfloat16)

    def low_of(phase):
        return stacked(low_sum(phase))

    def up_cols(begin, size):
        return up_got[:, :, begin : begin + size].reshape(requests * rank, size)

    cosine = cos_in[...]
    sine = sin_in[...]

    def rotated(u):
        return u * cosine + pltpu.roll(u, rank, 1) * sine

    scale = head_dim ** (-0.5) * 1.4426950408889634
    group = 4 * rows
    groups = range(head_count * rows // group)

    def cached(j, g):
        at = slice(g * group, (g + 1) * group)
        scores = (
            lax.dot_general(
                queries[j, at, :], kv_all[j, :, :head_dim], contract, preferred_element_type=jnp.float32
            )
            * scale
        )
        m = jnp.max(scores, axis=1, keepdims=True)
        w = jnp.exp2(scores - m)
        top[j, at, :] = jnp.broadcast_to(m, (group, head_dim))
        total[j, at, :] = jnp.broadcast_to(jnp.sum(w, axis=1, keepdims=True), (group, head_dim))
        acc[j, at, :] = jnp.dot(
            w.astype(jnp.bfloat16), kv_all[j, :, head_dim:], preferred_element_type=jnp.float32
        )

    def drain(p):
        across(p, 0, own[p]).wait_send()

        @pl.when(at_end)
        def _():
            z_copy(0, p, 0, to_first, own[p]).wait_send()
            if p in whole:
                for chip in range(1, 4):
                    across(p, chip).wait_send()

        @pl.when(inner)
        def _():
            z_copy(1, p, 0, to_second, own[p]).wait_send()
            z_copy(2, p, 1, to_second).wait_send()
            for chip in range(1, 4):
                across(p, chip).wait_send()
            if p in whole:
                z_copy(3, p, 0, to_first, own[p]).wait_send()
                z_copy(4, p, 2, to_first).wait_send()
                z_copy(5, p, 3, to_first).wait_send()
            else:
                z_sel(p, to_first).wait_send()

    def drain_spread(src, args):
        for j in range(requests):
            for k in (1, 2):
                spread(src, *args, j, k).wait_send()
            pass_on(*args, j).wait_send()

    relay(0)
    from_second(0)
    relay(1)
    from_second(1)
    relay(2)
    from_third(0)
    relay(3)
    from_third(1)
    relay(4)
    finish_inner(2)
    finish_end(0)
    finish_end(1)
    for j in range(requests):
        up_sel[j] = bufs[up_piece][wanted[j]]
    for j in range(requests):
        for k in (1, 2):
            spread(up_sel, *up_args, j, k).start()
        up_got[j, pl.ds(pl.multiple_of(seq * up_rows, up_rows), up_rows)] = up_sel[j]
    for k in (1, 2):
        spread(cache_in, *kv_args, 0, k).start()
    for p in range(3, 7):
        relay(p + 2)
        finish_inner(p)
    for p in range(9, count):
        relay(p)

    for copy in local[count:]:
        copy.wait()
    for k in others:
        hid_copy(k).wait_recv()
    finish_inner(7)
    for p in phases[0][1:]:
        finish_end(p)
    low_parts(0)
    for j in range(requests):
        spread(up_sel, *up_args, j, 1 + j).wait_recv()
        pass_on(*up_args, j).start()
    for k in (1, 2):
        spread(cache_in, *kv_args, 1, k).start()
    finish_inner(8)
    spread(cache_in, *kv_args, 0, 1).wait_recv()
    pass_on(*kv_args, 0).start()

    finish_inner(out_piece)
    finish_inner(10)
    low_q = low_of(0)
    for j in range(requests):
        spread(up_sel, *up_args, j, 2 - j).wait_recv()
        pass_on(*up_args, j).wait_recv()
    delta_q = jnp.dot(low_q, up_cols(0, q_width), preferred_element_type=jnp.float32)
    for j in range(requests):
        for h in range(head_count):
            cols = slice(h * head_dim, (h + 1) * head_dim)
            u = q_base[j, :, cols].astype(jnp.float32) + delta_q[j * rows : (j + 1) * rows, cols]
            queries[j, h * rows : (h + 1) * rows, :] = rotated(u).astype(jnp.bfloat16)
    for p in phases[1]:
        finish_end(p)
    low_parts(1)
    spread(cache_in, *kv_args, 1, 2).wait_recv()
    pass_on(*kv_args, 1).start()
    finish_end(out_piece)
    for j in range(requests):
        out_sel[j] = bufs[out_piece][mine[j]]
    for j in range(requests):
        for k in (1, 2):
            spread(out_sel, *out_args, j, k).start()
        out_got[j, pl.ds(pl.multiple_of(seq * up_rows, up_rows), up_rows)] = out_sel[j]
    finish_inner(11)
    finish_inner(12)
    spread(cache_in, *kv_args, 0, 2).wait_recv()
    pass_on(*kv_args, 0).wait_recv()
    for g in groups:
        cached(0, g)

    low_k = low_of(1)
    delta_k = jnp.dot(low_k, up_cols(q_width, head_dim), preferred_element_type=jnp.float32)
    for j in range(requests):
        at = slice(j * rows, (j + 1) * rows)
        key = rotated(kv_base[j, :, :head_dim].astype(jnp.float32) + delta_k[at]).astype(jnp.bfloat16)
        new_kv[j, :, :head_dim] = key
        key_new[j, pl.ds(pl.multiple_of(seq * rows, rows), rows), :] = key
    for k in others:
        new_copy(k).start()
    for k in others:
        base_copy(k).start()
    finish_inner(13)
    for p in range(8):
        drain(p)
    for k in others:
        hid_copy(k).wait_send()
    spread(cache_in, *kv_args, 1, 1).wait_recv()
    pass_on(*kv_args, 1).wait_recv()
    for g in groups:
        cached(1, g)
    for j in range(requests):
        spread(out_sel, *out_args, j, 1 + j).wait_recv()
        pass_on(*out_args, j).start()
    for p in phases[2]:
        finish_end(p)
    low_parts(2)
    for k in others:
        new_copy(k).wait_recv()
    token = lax.rem(lax.broadcasted_iota(jnp.int32, (group, span), 0), rows) + seq * rows
    visible = lax.broadcasted_iota(jnp.int32, (group, span), 1) <= token

    def in_span(j):
        for g in groups:
            at = slice(g * group, (g + 1) * group)
            scores = (
                lax.dot_general(
                    queries[j, at, :], key_new[j], contract, preferred_element_type=jnp.float32
                )
                * scale
            )
            scores = jnp.where(visible, scores, masked_score)
            old = top[j, at, :]
            m = jnp.maximum(old, jnp.max(scores, axis=1, keepdims=True))
            w = jnp.exp2(scores - m[:, :1])
            factor = jnp.exp2(old - m)
            denom = total[j, at, :] * factor + jnp.sum(w, axis=1, keepdims=True)
            total[j, at, :] = denom
            acc[j, at, :] = acc[j, at, :] * factor
            fresh[j, at, :] = w.astype(jnp.bfloat16)

    in_span(0)
    in_span(1)
    last = count - 1
    finish_end(last)
    tail = pieces[last][2]
    for j in range(requests):
        h = hid[:, j].reshape(span, depth)
        last_all[seq, j * tail : (j + 1) * tail, :] = lax.dot_general(
            bufs[last][mine[j]], h, contract, preferred_element_type=jnp.float32
        )
    for k in others:
        last_copy(k).start()
    low_all[pl.ds(pl.multiple_of(seq * rows, rows), rows), :] = low_sum(2).astype(jnp.bfloat16)
    for k in others:
        low_copy(k).start()
    for p in range(8, count):
        drain(p)
    for src, args in ((cache_in, kv_args), (up_sel, up_args), (out_sel, out_args)):
        drain_spread(src, args)
    for k in others:
        new_copy(k).wait_send()
        base_copy(k).wait_send()
        for phase in range(3):
            part_copy(phase, k).wait_send()
    for j in range(requests):
        spread(out_sel, *out_args, j, 2 - j).wait_recv()
        pass_on(*out_args, j).wait_recv()
    for k in others:
        base_copy(k).wait_recv()
    up_v = up_cols(q_width + head_dim, head_dim)
    for k in others:
        last_copy(k).wait_recv()
    low_last = last_all[0]
    for s in range(1, seq_count):
        low_last = low_last + last_all[s]
    up_last = jnp.concatenate(
        [up_v[(j + 1) * rank - tail : (j + 1) * rank] for j in range(requests)], axis=0
    )
    delta_last = jnp.dot(stacked(low_last.T), up_last, preferred_element_type=jnp.float32)
    for k in others:
        low_copy(k).wait_recv()
    low_v = stacked(low_all[...].astype(jnp.float32))
    delta_v = jnp.dot(low_v, up_v, preferred_element_type=jnp.float32) + delta_last
    for j in range(requests):
        value = base_all[j].astype(jnp.float32) + delta_v[j * span : (j + 1) * span]
        value_new[j] = value.astype(jnp.bfloat16)
    for j in range(requests):
        mixed = acc[j] + jnp.dot(fresh[j], value_new[j], preferred_element_type=jnp.float32)
        mixed = (mixed / total[j]).astype(jnp.bfloat16)
        for h in range(head_count):
            attn_out[j, :, h * head_dim : (h + 1) * head_dim] = mixed[h * rows : (h + 1) * rows]
        new_kv[j, :, head_dim:] = value_new[j, pl.ds(pl.multiple_of(seq * rows, rows), rows), :]
    for j in range(requests):
        o_low[j] = lax.dot_general(
            attn_out[j], out_got[j], contract, preferred_element_type=jnp.float32
        )

    for k in others:
        low_copy(k).wait_send()
        last_copy(k).wait_send()


def fused(
    hidden_in, q_base, kv_base, cache_kv, req_adapter, slot_of_adapter, down_panels, up_panels
):
    requests, rows, _ = hidden_in.shape
    head_dim = kv_base.shape[2] // 2
    q_width = q_base.shape[2]
    pre_rows = cache_kv.shape[1]
    seq_count = lax.axis_size("seq")
    req_count = lax.axis_size("req")
    depth = down_panels.shape[1]
    rank_rows, up_width = up_panels.shape[1:]
    half_dim = head_dim // 2
    panel = down_panels[0].T
    positions = (
        pre_rows * seq_count
        + lax.axis_index("seq") * rows
        + jnp.arange(rows, dtype=jnp.int32)
    )
    inverse = 500000.0 ** (-jnp.arange(half_dim, dtype=jnp.float32) / half_dim)
    angles = positions.astype(jnp.float32)[:, None] * inverse[None, :]
    cosine = jnp.cos(angles)
    sine = jnp.sin(angles)
    cosine = jnp.concatenate([cosine, cosine], axis=1)
    sine = jnp.concatenate([-sine, sine], axis=1)
    span = seq_count * rows
    q_rows = q_width // head_dim * rows
    bf16, f32 = jnp.bfloat16, jnp.float32
    dma = pltpu.SemaphoreType.DMA
    smem = pl.BlockSpec(memory_space=pltpu.SMEM)
    vmem = pl.BlockSpec(memory_space=pltpu.VMEM)
    anywhere = pl.BlockSpec(memory_space=pltpu.HBM)
    t = half_dim // 4
    up_part = q_width + 2 * head_dim
    pieces = [("down", i * t, t) for i in range(12)]
    pieces.insert(1, ("up", 0, up_part))
    pieces.insert(9, ("up", up_part, up_width - up_part))
    phases = ((0, 2, 3, 4), (5, 6, 7, 8), (10, 11, 12))
    count = len(pieces)
    shapes = [(rank_rows, n) if kind == "up" else (n, depth) for kind, _, n in pieces]
    return pl.pallas_call(
        functools.partial(attend_kernel, pieces, phases),
        out_shape=(
            jax.ShapeDtypeStruct((requests, rows, q_width), bf16),
            jax.ShapeDtypeStruct((requests, rows, half_dim), f32),
            jax.ShapeDtypeStruct((requests, rows, 2 * head_dim), bf16),
        ),
        in_specs=[smem, smem] + [anywhere] * 6 + [vmem, vmem],
        out_specs=(vmem, vmem, vmem),
        scratch_shapes=[
            pltpu.VMEM((requests, rows, q_width), bf16),
            pltpu.VMEM((requests, rows, 2 * head_dim), bf16),
            pltpu.VMEM((seq_count, requests, rows, depth), bf16),
            pltpu.VMEM((requests, rank_rows, up_part), bf16),
            pltpu.VMEM((requests, half_dim, up_part), bf16),
            pltpu.VMEM((requests, rank_rows, up_width - up_part), bf16),
            pltpu.VMEM((requests, half_dim, up_width - up_part), bf16),
            pltpu.VMEM((requests, seq_count * pre_rows, 2 * head_dim), bf16),
            pltpu.VMEM((requests, span, head_dim), bf16),
            pltpu.VMEM((requests, span, head_dim), bf16),
            pltpu.VMEM((3, seq_count, rows, head_dim), f32),
            pltpu.VMEM((3, seq_count, rows, head_dim), f32),
            pltpu.VMEM((requests, span, head_dim), bf16),
            pltpu.VMEM((span, head_dim), bf16),
            pltpu.VMEM((seq_count, requests * t, span), f32),
            pltpu.VMEM((requests, q_rows, head_dim), bf16),
            pltpu.VMEM((requests, q_rows, head_dim), f32),
            pltpu.VMEM((requests, q_rows, head_dim), f32),
            pltpu.VMEM((requests, q_rows, head_dim), f32),
            pltpu.VMEM((requests, q_rows, span), bf16),
            dma((count + 5,)),
        ]
        + [dma((6, count))] * 2
        + [dma((4, count))] * 2
        + [dma((seq_count,))] * 2
        + [dma((requests, seq_count))] * 6
        + [dma((3, seq_count))] * 2
        + [dma((seq_count,))] * 8
        + [pltpu.VMEM((req_count,) + shape, bf16) for shape in shapes]
        + [pltpu.VMEM((requests,) + shape, bf16) for shape in shapes],
        compiler_params=pltpu.CompilerParams(
            collective_id=0, has_side_effects=True, vmem_limit_bytes=48 * 1024 * 1024
        ),
    )(
        *[
            pltpu.with_memory_space_constraint(a, pltpu.HBM)
            for a in (
                req_adapter,
                slot_of_adapter,
                hidden_in,
                panel,
                up_panels[0],
                cache_kv,
                q_base,
                kv_base,
            )
        ],
        cosine,
        sine,
    )


def fits(mesh, hidden_in, down_panels):
    return (
        mesh.shape["req"] == 8
        and mesh.shape["seq"] == 4
        and hidden_in.shape[0] == 2
        and down_panels.shape[0] == 1
        and down_panels.shape[2] == 192
    )


def solution(mesh):
    def body(*arrays):
        return (fused if fits(mesh, arrays[0], arrays[6]) else on_device)(*arrays)

    return jax.shard_map(
        body,
        mesh=mesh,
        in_specs=(
            P("req", "seq", None),
            P("req", "seq", None),
            P("req", "seq", None),
            P("req", "seq", None),
            P(),
            P(),
            P("req", "seq", None),
            P("req", "seq", None),
        ),
        out_specs=(P("req", "seq", None), P("req", "seq", None), P("req", "seq", None)),
        check_vma=False,
    )
```

```python
import functools

import jax
import jax.numpy as jnp
from jax import lax
from jax.experimental import pallas as pl
from jax.experimental.pallas import tpu as pltpu
from jax.sharding import PartitionSpec as P

masked_score = -1e30
MESH = pl.DeviceIdType.MESH


def rotate(vectors, positions):
    half_dim = vectors.shape[-1] // 2
    inverse = 500000.0 ** (-jnp.arange(half_dim, dtype=jnp.float32) / half_dim)
    angles = positions.astype(jnp.float32)[:, None] * inverse[None, :]
    cosine = jnp.cos(angles)[:, None, :]
    sine_part = jnp.sin(angles)[:, None, :]
    first_half = vectors[..., :half_dim]
    second_half = vectors[..., half_dim:]
    return jnp.concatenate(
        [
            first_half * cosine - second_half * sine_part,
            second_half * cosine + first_half * sine_part,
        ],
        axis=-1,
    )


def on_device(
    hidden_in, q_base, kv_base, cache_kv, req_adapter, slot_of_adapter, down_panels, up_panels
):
    requests, seg_rows, model_width = hidden_in.shape
    head_dim = kv_base.shape[2] // 2
    q_width = q_base.shape[2]
    head_count = q_width // head_dim
    rank_all = down_panels.shape[2]
    rank_size = rank_all // 3
    pre_rows = cache_kv.shape[1]
    seq_count = lax.axis_size("seq")
    seq_pos = lax.axis_index("seq")
    req_pos = lax.axis_index("req")
    context = pre_rows * seq_count
    my_adapters = lax.dynamic_slice_in_dim(req_adapter, req_pos * requests, requests)
    wanted = jnp.take(slot_of_adapter, my_adapters)
    pieces = (
        lax.all_gather(down_panels, "req", axis=0, tiled=True),
        lax.all_gather(up_panels, "req", axis=0, tiled=True),
    )
    slot_ids = jnp.arange(pieces[0].shape[0], dtype=jnp.int32)
    onehot = (wanted[:, None] == slot_ids[None, :]).astype(jnp.bfloat16)
    down_part = jnp.einsum("js,snc->jnc", onehot, pieces[0], preferred_element_type=jnp.float32)
    up_part = jnp.einsum("js,snc->jnc", onehot, pieces[1], preferred_element_type=jnp.float32)
    down_sel = down_part
    up_sel = up_part
    down_sel = down_sel.astype(jnp.bfloat16)
    up_sel = up_sel.astype(jnp.bfloat16)
    up_full = lax.all_gather(up_sel, "seq", axis=1, tiled=True)
    low_rank = jnp.einsum(
        "jtd,jdc->jtc",
        hidden_in,
        lax.all_gather(down_sel, "seq", axis=1, tiled=True),
        preferred_element_type=jnp.float32,
    )
    low_half = low_rank.astype(jnp.bfloat16)
    delta_q = jnp.einsum(
        "jtr,jrc->jtc",
        low_half[:, :, :rank_size],
        up_full[:, :, :q_width],
        preferred_element_type=jnp.float32,
    )
    delta_k = jnp.einsum(
        "jtr,jrc->jtc",
        low_half[:, :, rank_size : 2 * rank_size],
        up_full[:, :, q_width : q_width + head_dim],
        preferred_element_type=jnp.float32,
    )
    delta_v = jnp.einsum(
        "jtr,jrc->jtc",
        low_half[:, :, 2 * rank_size :],
        up_full[:, :, q_width + head_dim : q_width + 2 * head_dim],
        preferred_element_type=jnp.float32,
    )
    query_index = seq_pos * seg_rows + jnp.arange(seg_rows, dtype=jnp.int32)
    positions = context + query_index
    queries = rotate(
        (q_base.astype(jnp.float32) + delta_q).reshape(requests, seg_rows, head_count, head_dim),
        positions,
    ).astype(jnp.bfloat16)
    keys_new = rotate(
        (kv_base[:, :, :head_dim].astype(jnp.float32) + delta_k)[:, :, None, :], positions
    )[:, :, 0, :]
    values_new = kv_base[:, :, head_dim:].astype(jnp.float32) + delta_v
    new_kv = jnp.concatenate([keys_new, values_new], axis=2).astype(jnp.bfloat16)
    local_kv = jnp.concatenate([cache_kv, new_kv], axis=1)
    kv_rows = pre_rows + seg_rows
    score_scale = head_dim ** (-0.5)

    def attend_block(state_now, key_block, first_row):
        running_max, running_sum, weighted = state_now
        key_part = key_block[:, :, :head_dim]
        value_part = key_block[:, :, head_dim:]
        scores = (
            jnp.einsum("jthd,jkd->jhtk", queries, key_part, preferred_element_type=jnp.float32)
            * score_scale
        )
        global_index = first_row + jnp.arange(key_block.shape[1], dtype=jnp.int32)
        owner_dev = global_index // kv_rows
        offset = global_index % kv_rows
        span_index = owner_dev * seg_rows + offset - pre_rows
        visible = (offset[None, :] < pre_rows) | (span_index[None, :] <= query_index[:, None])
        scores = jnp.where(visible[None, None], scores, masked_score)
        newest = jnp.maximum(running_max, jnp.max(scores, axis=-1))
        weights = jnp.where(visible[None, None], jnp.exp(scores - newest[..., None]), 0.0)
        factor = jnp.exp(running_max - newest)
        running_sum = running_sum * factor + jnp.sum(weights, axis=-1)
        weighted = weighted * factor[..., None] + jnp.einsum(
            "jhtk,jkd->jhtd",
            weights.astype(jnp.bfloat16),
            value_part,
            preferred_element_type=jnp.float32,
        )
        return (newest, running_sum, weighted)

    start_state = (
        jnp.full((requests, head_count, seg_rows), masked_score, jnp.float32),
        jnp.zeros((requests, head_count, seg_rows), jnp.float32),
        jnp.zeros((requests, head_count, seg_rows, head_dim), jnp.float32),
    )
    kv_piece = lax.all_gather(local_kv, "seq", axis=1, tiled=True)
    piece_rows = kv_piece.shape[1]

    def advance(block_number, state_inner):
        key_block = lax.dynamic_slice_in_dim(kv_piece, block_number * kv_rows, kv_rows, 1)
        return attend_block(state_inner, key_block, block_number * kv_rows)

    running_max, running_sum, weighted = lax.fori_loop(
        0, piece_rows // kv_rows, advance, start_state
    )
    mixed = weighted / running_sum[..., None]
    attn_out = (
        jnp.transpose(mixed, (0, 2, 1, 3)).reshape(requests, seg_rows, q_width).astype(jnp.bfloat16)
    )
    o_low = jnp.einsum(
        "jtc,jrc->jtr",
        attn_out,
        up_full[:, :, q_width + 2 * head_dim :],
        preferred_element_type=jnp.float32,
    )
    return (attn_out, o_low, new_kv)

def attend_kernel(
    pieces,
    phases,
    req_adapter,
    slot_of_adapter,
    hidden_in,
    down_in,
    up_in,
    cache_in,
    q_in,
    kv_in,
    cos_in,
    sin_in,
    attn_out,
    o_low,
    new_kv,
    q_base,
    kv_base,
    hid,
    up_sel,
    up_got,
    out_sel,
    out_got,
    kv_all,
    key_new,
    value_new,
    part,
    part_got,
    base_all,
    low_all,
    last_all,
    queries,
    acc,
    top,
    total,
    fresh,
    local_sem,
    z_send,
    z_recv,
    mate_send,
    mate_recv,
    hid_send,
    hid_recv,
    kv_send,
    kv_recv,
    up_send,
    up_recv,
    out_send,
    out_recv,
    part_send,
    part_recv,
    new_send,
    new_recv,
    base_send,
    base_recv,
    low_send,
    low_recv,
    last_send,
    last_recv,
    *panels,
):
    requests, rows, _ = q_base.shape
    seq_count, _, _, depth = hid.shape
    head_dim = kv_base.shape[2] // 2
    q_width = q_base.shape[2]
    head_count = q_width // head_dim
    rank = head_dim // 2
    pre_rows = cache_in.shape[1]
    up_rows = up_in.shape[0]
    span = seq_count * rows
    count = len(pieces)
    bufs, stages = panels[:count], panels[count:]
    up_piece, out_piece = [p for p in range(count) if pieces[p][0] == "up"]
    whole = (0, up_piece)
    seq = lax.axis_index("seq")
    req = lax.axis_index("req")
    z = req // 2
    core = req % 2
    at_end = (z == 0) | (z == 3)
    inner = jnp.logical_not(at_end)
    left = z < 2
    first = jnp.where(z == 0, 1, jnp.where(z == 1, 0, jnp.where(z == 2, 3, 2)))
    second = jnp.where(at_end, 3 - first, 3 - z)
    third = jnp.where(at_end, 3 - z, 3 - first)
    chips = (z, first, second, third)
    slots = [chip * 2 + core for chip in chips]
    land = jnp.where(left, 2, 0)
    mate = {"req": z * 2 + (1 - core)}
    to_first = {"req": slots[1]}
    to_second = {"req": slots[2]}
    peers = [seq, seq + 1 - 2 * (seq % 2), (seq + 2) % 4, 3 - seq]
    others = range(1, seq_count)

    def send(src, dst, s_sem, r_sem, target):
        return pltpu.make_async_remote_copy(
            src_ref=src,
            dst_ref=dst,
            send_sem=s_sem,
            recv_sem=r_sem,
            device_id=target,
            device_id_type=MESH,
        )

    own = [
        up_in.at[:, pl.ds(begin, size)] if kind == "up" else down_in.at[pl.ds(begin, size)]
        for kind, begin, size in pieces
    ]
    local = [pltpu.make_async_copy(own[p], bufs[p].at[slots[0]], local_sem.at[p]) for p in range(count)]
    local.append(
        pltpu.make_async_copy(
            hidden_in.at[:, :, pl.ds(seq * depth, depth)], hid.at[seq], local_sem.at[count]
        )
    )
    local.append(
        pltpu.make_async_copy(
            cache_in, kv_all.at[:, pl.ds(seq * pre_rows, pre_rows), :], local_sem.at[count + 1]
        )
    )

    local.append(
        pltpu.make_async_copy(
            kv_in.at[:, :, pl.ds(head_dim, head_dim)],
            base_all.at[:, pl.ds(pl.multiple_of(seq * rows, rows), rows), :],
            local_sem.at[count + 4],
        )
    )
    local.append(pltpu.make_async_copy(q_in, q_base, local_sem.at[count + 2]))
    local.append(pltpu.make_async_copy(kv_in, kv_base, local_sem.at[count + 3]))

    barrier = pltpu.get_barrier_semaphore()
    for k in others:
        pl.semaphore_signal(barrier, inc=1, device_id={"seq": peers[k]}, device_id_type=MESH)
    pl.semaphore_signal(barrier, inc=1, device_id=mate, device_id_type=MESH)
    pl.semaphore_signal(barrier, inc=1, device_id=to_first, device_id_type=MESH)

    @pl.when(inner)
    def _():
        pl.semaphore_signal(barrier, inc=1, device_id=to_second, device_id_type=MESH)

    pl.semaphore_wait(barrier, seq_count + 1 + inner.astype(jnp.int32))

    def z_copy(kind, p, chip, target, src=None):
        here = bufs[p].at[slots[chip]]
        return send(here if src is None else src, here, z_send.at[kind, p], z_recv.at[kind, p], target)

    def z_sel(p, target):
        return send(
            stages[p], bufs[p].at[pl.ds(land, requests)], z_send.at[3, p], z_recv.at[3, p], target
        )

    def across(p, chip, src=None):
        here = bufs[p].at[slots[chip]]
        return send(
            here if src is None else src, here, mate_send.at[chip, p], mate_recv.at[chip, p], mate
        )

    def hid_copy(k):
        return send(
            hidden_in.at[:, :, pl.ds(peers[k] * depth, depth)],
            hid.at[seq],
            hid_send.at[k],
            hid_recv.at[k],
            {"seq": peers[k]},
        )

    def spread(src, dst, size, sems, j, k):
        at = pl.ds(pl.multiple_of(seq * size, size), size)
        return send(src.at[j], dst.at[j, at], sems[0].at[j, k], sems[1].at[j, k], {"seq": peers[k]})

    def pass_on(dst, size, sems, j):
        here = dst.at[j, pl.ds(pl.multiple_of(peers[1 + j] * size, size), size)]
        return send(here, here, sems[0].at[j, 3], sems[1].at[j, 3], {"seq": peers[2 - j]})

    kv_args = (kv_all, pre_rows, (kv_send, kv_recv))
    up_args = (up_got, up_rows, (up_send, up_recv))
    out_args = (out_got, up_rows, (out_send, out_recv))

    def part_copy(phase, k):
        return send(
            part.at[phase, peers[k]],
            part_got.at[phase, k],
            part_send.at[phase, k],
            part_recv.at[phase, k],
            {"seq": peers[k]},
        )

    def new_copy(k):
        here = key_new.at[:, pl.ds(pl.multiple_of(seq * rows, rows), rows), :]
        return send(here, here, new_send.at[k], new_recv.at[k], {"seq": peers[k]})

    def base_copy(k):
        return send(
            kv_in.at[:, :, pl.ds(head_dim, head_dim)],
            base_all.at[:, pl.ds(pl.multiple_of(seq * rows, rows), rows), :],
            base_send.at[k],
            base_recv.at[k],
            {"seq": peers[k]},
        )

    def low_copy(k):
        here = low_all.at[pl.ds(pl.multiple_of(seq * rows, rows), rows)]
        return send(here, here, low_send.at[k], low_recv.at[k], {"seq": peers[k]})

    def last_copy(k):
        here = last_all.at[seq]
        return send(here, here, last_send.at[k], last_recv.at[k], {"seq": peers[k]})

    @pl.when(at_end)
    def _():
        for p in range(2):
            z_copy(0, p, 0, to_first, own[p]).start()

    @pl.when(inner)
    def _():
        for p in range(3):
            z_copy(1, p, 0, to_second, own[p]).start()
            if p in whole:
                z_copy(3, p, 0, to_first, own[p]).start()

    for k in (3, 1, 2):
        hid_copy(k).start()

    @pl.when(at_end)
    def _():
        for p in range(2, count):
            z_copy(0, p, 0, to_first, own[p]).start()

    for copy in local:
        copy.start()
    for p in range(count):
        across(p, 0, own[p]).start()

    wanted = [slot_of_adapter[req_adapter[req * requests + j]] for j in range(requests)]
    mine = [
        jnp.where(at_end & (w // 2 != z), land + j, w) for j, w in enumerate(wanted)
    ]

    def relay(p):
        @pl.when(inner)
        def _():
            z_copy(0, p, 1, to_first).wait_recv()
            z_copy(2, p, 1, to_second).start()
            across(p, 1).start()
            ahead = 3 if p == 0 else p + 2
            if p != 1 and ahead < count:
                z_copy(1, ahead, 0, to_second, own[ahead]).start()

    def from_second(p):
        @pl.when(inner)
        def _():
            z_copy(1, p, 2, to_second).wait_recv()
            across(p, 2).start()
            if p in whole:
                z_copy(4, p, 2, to_first).start()

    def from_third(p):
        @pl.when(inner)
        def _():
            z_copy(2, p, 3, to_second).wait_recv()
            across(p, 3).start()
            if p in whole:
                z_copy(5, p, 3, to_first).start()
            local[p].wait()
            for chip in range(4):
                across(p, chip).wait_recv()
            if p not in whole:
                for j in range(requests):
                    w = slot_of_adapter[req_adapter[slots[1] * requests + j]]
                    w = jnp.where(w // 2 == first, slots[0], w)
                    stages[p][j] = bufs[p][w]
                z_sel(p, to_first).start()

    def finish_inner(p):
        from_second(p)
        from_third(p)

    def finish_end(p):
        @pl.when(at_end)
        def _():
            if p in whole:
                for kind in range(3):
                    z_copy(3 + kind, p, 1 + kind, to_first).wait_recv()
                    across(p, 1 + kind).start()
            else:
                z_sel(p, to_first).wait_recv()
            local[p].wait()
            for chip in range(4 if p in whole else 1):
                across(p, chip).wait_recv()

    contract = (((1,), (1,)), ((), ()))

    def low_parts(phase):
        thin = []
        for j in range(requests):
            panel = [bufs[p][wanted[j] if p in whole else mine[j]] for p in phases[phase]]
            short = rank - sum(pieces[p][2] for p in phases[phase])
            if short:
                panel.append(jnp.zeros((short, depth), jnp.bfloat16))
            panel = jnp.concatenate(panel, axis=0)
            h = hid[:, j].reshape(span, depth)
            thin.append(lax.dot_general(h, panel, contract, preferred_element_type=jnp.float32))
        joined = jnp.concatenate(thin, axis=1)
        for s in range(seq_count):
            part[phase, s] = joined[s * rows : (s + 1) * rows]
        for k in others:
            part_copy(phase, k).start()

    def low_sum(phase):
        for k in others:
            part_copy(phase, k).wait_recv()
        low = part[phase, seq]
        for k in others:
            low = low + part_got[phase, k]
        return low

    def stacked(low):
        size, width = low.shape
        low = jnp.concatenate([low] * requests, axis=0)
        row = lax.broadcasted_iota(jnp.int32, low.shape, 0) // size
        lane = lax.broadcasted_iota(jnp.int32, low.shape, 1) // (width // requests)
        return jnp.where(row == lane, low, 0.0).astype(jnp.bfloat16)

    def low_of(phase):
        return stacked(low_sum(phase))

    def up_cols(begin, size):
        return up_got[:, :, begin : begin + size].reshape(requests * rank, size)

    cosine = cos_in[...]
    sine = sin_in[...]

    def rotated(u):
        return u * cosine + pltpu.roll(u, rank, 1) * sine

    scale = head_dim ** (-0.5) * 1.4426950408889634
    group = 8 * rows
    groups = range(head_count * rows // group)

    def cached(j, g):
        at = slice(g * group, (g + 1) * group)
        scores = (
            lax.dot_general(
                queries[j, at, :], kv_all[j, :, :head_dim], contract, preferred_element_type=jnp.float32
            )
            * scale
        )
        m = jnp.max(scores, axis=1, keepdims=True)
        w = jnp.exp2(scores - m)
        top[j, at, :] = jnp.broadcast_to(m, (group, head_dim))
        total[j, at, :] = jnp.broadcast_to(jnp.sum(w, axis=1, keepdims=True), (group, head_dim))
        acc[j, at, :] = jnp.dot(
            w.astype(jnp.bfloat16), kv_all[j, :, head_dim:], preferred_element_type=jnp.float32
        )

    def drain(p):
        across(p, 0, own[p]).wait_send()

        @pl.when(at_end)
        def _():
            z_copy(0, p, 0, to_first, own[p]).wait_send()
            if p in whole:
                for chip in range(1, 4):
                    across(p, chip).wait_send()

        @pl.when(inner)
        def _():
            z_copy(1, p, 0, to_second, own[p]).wait_send()
            z_copy(2, p, 1, to_second).wait_send()
            for chip in range(1, 4):
                across(p, chip).wait_send()
            if p in whole:
                z_copy(3, p, 0, to_first, own[p]).wait_send()
                z_copy(4, p, 2, to_first).wait_send()
                z_copy(5, p, 3, to_first).wait_send()
            else:
                z_sel(p, to_first).wait_send()

    def drain_spread(src, args):
        for j in range(requests):
            for k in (1, 2):
                spread(src, *args, j, k).wait_send()
            pass_on(*args, j).wait_send()

    relay(0)
    from_second(0)
    relay(1)
    from_second(1)
    relay(2)
    from_third(0)
    relay(3)
    from_third(1)
    relay(4)
    finish_inner(2)
    finish_end(0)
    finish_end(1)
    for j in range(requests):
        up_sel[j] = bufs[up_piece][wanted[j]]
    for j in range(requests):
        for k in (1, 2):
            spread(up_sel, *up_args, j, k).start()
        up_got[j, pl.ds(pl.multiple_of(seq * up_rows, up_rows), up_rows)] = up_sel[j]
    for k in (1, 2):
        spread(cache_in, *kv_args, 0, k).start()
    for p in range(3, 7):
        relay(p + 2)
        finish_inner(p)
    for p in range(9, count):
        relay(p)

    for copy in local[count:]:
        copy.wait()
    for k in others:
        hid_copy(k).wait_recv()
    finish_inner(7)
    for p in phases[0][1:]:
        finish_end(p)
    low_parts(0)
    for j in range(requests):
        spread(up_sel, *up_args, j, 1 + j).wait_recv()
        pass_on(*up_args, j).start()
    for k in (1, 2):
        spread(cache_in, *kv_args, 1, k).start()
    finish_inner(8)
    spread(cache_in, *kv_args, 0, 1).wait_recv()
    pass_on(*kv_args, 0).start()

    finish_inner(out_piece)
    finish_inner(10)
    low_q = low_of(0)
    for j in range(requests):
        spread(up_sel, *up_args, j, 2 - j).wait_recv()
        pass_on(*up_args, j).wait_recv()
    delta_q = jnp.dot(low_q, up_cols(0, q_width), preferred_element_type=jnp.float32)
    for j in range(requests):
        for h in range(head_count):
            cols = slice(h * head_dim, (h + 1) * head_dim)
            u = q_base[j, :, cols].astype(jnp.float32) + delta_q[j * rows : (j + 1) * rows, cols]
            queries[j, h * rows : (h + 1) * rows, :] = rotated(u).astype(jnp.bfloat16)
    for p in phases[1]:
        finish_end(p)
    low_parts(1)
    spread(cache_in, *kv_args, 1, 2).wait_recv()
    pass_on(*kv_args, 1).start()
    finish_end(out_piece)
    for j in range(requests):
        out_sel[j] = bufs[out_piece][mine[j]]
    for j in range(requests):
        for k in (1, 2):
            spread(out_sel, *out_args, j, k).start()
        out_got[j, pl.ds(pl.multiple_of(seq * up_rows, up_rows), up_rows)] = out_sel[j]
    finish_inner(11)
    finish_inner(12)
    spread(cache_in, *kv_args, 0, 2).wait_recv()
    pass_on(*kv_args, 0).wait_recv()
    for g in groups:
        cached(0, g)

    finish_inner(13)
    low_k = low_of(1)
    delta_k = jnp.dot(low_k, up_cols(q_width, head_dim), preferred_element_type=jnp.float32)
    for j in range(requests):
        at = slice(j * rows, (j + 1) * rows)
        key = rotated(kv_base[j, :, :head_dim].astype(jnp.float32) + delta_k[at]).astype(jnp.bfloat16)
        new_kv[j, :, :head_dim] = key
        key_new[j, pl.ds(pl.multiple_of(seq * rows, rows), rows), :] = key
    for k in others:
        new_copy(k).start()
    for k in others:
        base_copy(k).start()
    for p in range(8):
        drain(p)
    for k in others:
        hid_copy(k).wait_send()
    spread(cache_in, *kv_args, 1, 1).wait_recv()
    pass_on(*kv_args, 1).wait_recv()
    for g in groups:
        cached(1, g)
    for j in range(requests):
        spread(out_sel, *out_args, j, 1 + j).wait_recv()
        pass_on(*out_args, j).start()
    for p in phases[2]:
        finish_end(p)
    low_parts(2)
    for k in others:
        new_copy(k).wait_recv()
    token = lax.rem(lax.broadcasted_iota(jnp.int32, (group, span), 0), rows) + seq * rows
    visible = lax.broadcasted_iota(jnp.int32, (group, span), 1) <= token

    def in_span(j):
        for g in groups:
            at = slice(g * group, (g + 1) * group)
            scores = (
                lax.dot_general(
                    queries[j, at, :], key_new[j], contract, preferred_element_type=jnp.float32
                )
                * scale
            )
            scores = jnp.where(visible, scores, masked_score)
            old = top[j, at, :]
            m = jnp.maximum(old, jnp.max(scores, axis=1, keepdims=True))
            w = jnp.exp2(scores - m[:, :1])
            factor = jnp.exp2(old - m)
            denom = total[j, at, :] * factor + jnp.sum(w, axis=1, keepdims=True)
            total[j, at, :] = denom
            acc[j, at, :] = acc[j, at, :] * factor
            fresh[j, at, :] = w.astype(jnp.bfloat16)

    in_span(0)
    in_span(1)
    last = count - 1
    finish_end(last)
    tail = pieces[last][2]
    for j in range(requests):
        h = hid[:, j].reshape(span, depth)
        last_all[seq, j * tail : (j + 1) * tail, :] = lax.dot_general(
            bufs[last][mine[j]], h, contract, preferred_element_type=jnp.float32
        )
    for k in others:
        last_copy(k).start()
    low_all[pl.ds(pl.multiple_of(seq * rows, rows), rows), :] = low_sum(2).astype(jnp.bfloat16)
    for k in others:
        low_copy(k).start()
    for p in range(8, count):
        drain(p)
    for src, args in ((cache_in, kv_args), (up_sel, up_args), (out_sel, out_args)):
        drain_spread(src, args)
    for k in others:
        new_copy(k).wait_send()
        base_copy(k).wait_send()
        for phase in range(3):
            part_copy(phase, k).wait_send()
    for j in range(requests):
        spread(out_sel, *out_args, j, 2 - j).wait_recv()
        pass_on(*out_args, j).wait_recv()
    for k in others:
        base_copy(k).wait_recv()
    up_v = up_cols(q_width + head_dim, head_dim)
    for k in others:
        last_copy(k).wait_recv()
    low_last = last_all[0]
    for s in range(1, seq_count):
        low_last = low_last + last_all[s]
    up_last = jnp.concatenate(
        [up_v[(j + 1) * rank - tail : (j + 1) * rank] for j in range(requests)], axis=0
    )
    delta_last = jnp.dot(stacked(low_last.T), up_last, preferred_element_type=jnp.float32)
    for k in others:
        low_copy(k).wait_recv()
    low_v = stacked(low_all[...].astype(jnp.float32))
    delta_v = jnp.dot(low_v, up_v, preferred_element_type=jnp.float32) + delta_last
    for j in range(requests):
        value = base_all[j].astype(jnp.float32) + delta_v[j * span : (j + 1) * span]
        value_new[j] = value.astype(jnp.bfloat16)
    for j in range(requests):
        mixed = acc[j] + jnp.dot(fresh[j], value_new[j], preferred_element_type=jnp.float32)
        mixed = (mixed / total[j]).astype(jnp.bfloat16)
        for h in range(head_count):
            attn_out[j, :, h * head_dim : (h + 1) * head_dim] = mixed[h * rows : (h + 1) * rows]
        new_kv[j, :, head_dim:] = value_new[j, pl.ds(pl.multiple_of(seq * rows, rows), rows), :]
    for j in range(requests):
        o_low[j] = lax.dot_general(
            attn_out[j], out_got[j], contract, preferred_element_type=jnp.float32
        )

    for k in others:
        low_copy(k).wait_send()
        last_copy(k).wait_send()


def fused(
    hidden_in, q_base, kv_base, cache_kv, req_adapter, slot_of_adapter, down_panels, up_panels
):
    requests, rows, _ = hidden_in.shape
    head_dim = kv_base.shape[2] // 2
    q_width = q_base.shape[2]
    pre_rows = cache_kv.shape[1]
    seq_count = lax.axis_size("seq")
    req_count = lax.axis_size("req")
    depth = down_panels.shape[1]
    rank_rows, up_width = up_panels.shape[1:]
    half_dim = head_dim // 2
    panel = down_panels[0].T
    positions = (
        pre_rows * seq_count
        + lax.axis_index("seq") * rows
        + jnp.arange(rows, dtype=jnp.int32)
    )
    inverse = 500000.0 ** (-jnp.arange(half_dim, dtype=jnp.float32) / half_dim)
    angles = positions.astype(jnp.float32)[:, None] * inverse[None, :]
    cosine = jnp.cos(angles)
    sine = jnp.sin(angles)
    cosine = jnp.concatenate([cosine, cosine], axis=1)
    sine = jnp.concatenate([-sine, sine], axis=1)
    span = seq_count * rows
    q_rows = q_width // head_dim * rows
    bf16, f32 = jnp.bfloat16, jnp.float32
    dma = pltpu.SemaphoreType.DMA
    smem = pl.BlockSpec(memory_space=pltpu.SMEM)
    vmem = pl.BlockSpec(memory_space=pltpu.VMEM)
    anywhere = pl.BlockSpec(memory_space=pltpu.HBM)
    t = half_dim // 4
    up_part = q_width + 2 * head_dim
    pieces = [("down", i * t, t) for i in range(12)]
    pieces.insert(1, ("up", 0, up_part))
    pieces.insert(9, ("up", up_part, up_width - up_part))
    phases = ((0, 2, 3, 4), (5, 6, 7, 8), (10, 11, 12))
    count = len(pieces)
    shapes = [(rank_rows, n) if kind == "up" else (n, depth) for kind, _, n in pieces]
    return pl.pallas_call(
        functools.partial(attend_kernel, pieces, phases),
        out_shape=(
            jax.ShapeDtypeStruct((requests, rows, q_width), bf16),
            jax.ShapeDtypeStruct((requests, rows, half_dim), f32),
            jax.ShapeDtypeStruct((requests, rows, 2 * head_dim), bf16),
        ),
        in_specs=[smem, smem] + [anywhere] * 6 + [vmem, vmem],
        out_specs=(vmem, vmem, vmem),
        scratch_shapes=[
            pltpu.VMEM((requests, rows, q_width), bf16),
            pltpu.VMEM((requests, rows, 2 * head_dim), bf16),
            pltpu.VMEM((seq_count, requests, rows, depth), bf16),
            pltpu.VMEM((requests, rank_rows, up_part), bf16),
            pltpu.VMEM((requests, half_dim, up_part), bf16),
            pltpu.VMEM((requests, rank_rows, up_width - up_part), bf16),
            pltpu.VMEM((requests, half_dim, up_width - up_part), bf16),
            pltpu.VMEM((requests, seq_count * pre_rows, 2 * head_dim), bf16),
            pltpu.VMEM((requests, span, head_dim), bf16),
            pltpu.VMEM((requests, span, head_dim), bf16),
            pltpu.VMEM((3, seq_count, rows, head_dim), f32),
            pltpu.VMEM((3, seq_count, rows, head_dim), f32),
            pltpu.VMEM((requests, span, head_dim), bf16),
            pltpu.VMEM((span, head_dim), bf16),
            pltpu.VMEM((seq_count, requests * t, span), f32),
            pltpu.VMEM((requests, q_rows, head_dim), bf16),
            pltpu.VMEM((requests, q_rows, head_dim), f32),
            pltpu.VMEM((requests, q_rows, head_dim), f32),
            pltpu.VMEM((requests, q_rows, head_dim), f32),
            pltpu.VMEM((requests, q_rows, span), bf16),
            dma((count + 5,)),
        ]
        + [dma((6, count))] * 2
        + [dma((4, count))] * 2
        + [dma((seq_count,))] * 2
        + [dma((requests, seq_count))] * 6
        + [dma((3, seq_count))] * 2
        + [dma((seq_count,))] * 8
        + [pltpu.VMEM((req_count,) + shape, bf16) for shape in shapes]
        + [pltpu.VMEM((requests,) + shape, bf16) for shape in shapes],
        compiler_params=pltpu.CompilerParams(
            collective_id=0, has_side_effects=True, vmem_limit_bytes=48 * 1024 * 1024
        ),
    )(
        *[
            pltpu.with_memory_space_constraint(a, pltpu.HBM)
            for a in (
                req_adapter,
                slot_of_adapter,
                hidden_in,
                panel,
                up_panels[0],
                cache_kv,
                q_base,
                kv_base,
            )
        ],
        cosine,
        sine,
    )


def fits(mesh, hidden_in, down_panels):
    return (
        mesh.shape["req"] == 8
        and mesh.shape["seq"] == 4
        and hidden_in.shape[0] == 2
        and down_panels.shape[0] == 1
        and down_panels.shape[2] == 192
    )


def solution(mesh):
    def body(*arrays):
        return (fused if fits(mesh, arrays[0], arrays[6]) else on_device)(*arrays)

    return jax.shard_map(
        body,
        mesh=mesh,
        in_specs=(
            P("req", "seq", None),
            P("req", "seq", None),
            P("req", "seq", None),
            P("req", "seq", None),
            P(),
            P(),
            P("req", "seq", None),
            P("req", "seq", None),
        ),
        out_specs=(P("req", "seq", None), P("req", "seq", None), P("req", "seq", None)),
        check_vma=False,
    )
```
